32 devices in a mesh: groups: 2 (over x), dp: 16 (over z, y, core).
Axes of the slice: x: 2, y: 2, z: 4, core: 2. Of those that a mesh axis runs over, the one named last changes fastest.
Arguments:
- res_lat: bfloat16 [256, 128, 512], P(('groups', 'dp')), parts along dimension 0, may hold values from -6 to 6
- res_rope: bfloat16 [256, 64, 128], P(('groups', 'dp')), parts along dimension 0, may hold values from -6 to 6
- res_table: int32 [32, 8], P(('groups', 'dp')), parts along dimension 0, may hold values from 0 to 7, each once within a row
- res_len: int32 [32], P(('groups', 'dp')), parts along dimension 0, may hold values from 1 to 1024
- out_lat: bfloat16 [256, 128, 512], P(('groups', 'dp')), parts along dimension 0, may hold values from -6 to 6
- out_rope: bfloat16 [256, 64, 128], P(('groups', 'dp')), parts along dimension 0, may hold values from -6 to 6
- out_fill: int32 [256], P(('groups', 'dp')), parts along dimension 0, may hold values from 1 to 128
- send_table: int32 [512], P(('groups', 'dp')), parts along dimension 0, may hold values from -1 to 7, as said below
- arr_index: int32 [480], P(('groups', 'dp')), parts along dimension 0, may hold values from 0 to 15, as said below
- arr_count: int32 [32], P(('groups', 'dp')), parts along dimension 0, may hold values from 1 to 15, as said below
- mig_lat: bfloat16 [384, 128, 512], P(('groups', 'dp')), parts along dimension 0, may hold values from -6 to 6
- mig_rope: bfloat16 [384, 64, 128], P(('groups', 'dp')), parts along dimension 0, may hold values from -6 to 6
- mig_len: int32 [32], P(('groups', 'dp')), parts along dimension 0, may hold values from 1 to 1536
- mig_bit: int32 [32], P(('groups', 'dp')), parts along dimension 0, may hold values from -1 to 3, as said below
- q_lat: bfloat16 [96, 4, 128, 512], P(('groups', 'dp')), parts along dimension 0, may hold values from -12 to 12
- q_rope: bfloat16 [96, 4, 64, 128], P(('groups', 'dp')), parts along dimension 0, may hold values from -6 to 6
- new_kv: bfloat16 [96, 4, 576], P(('groups', 'dp')), parts along dimension 0, may hold values from -6 to 6
Outputs:
- attended: bfloat16 [96, 4, 128, 512], P(('groups', 'dp')), parts along dimension 0
The draws below stay inside these ranges and needn't reach their ends.
There are 2 independent parts, one for each index of `groups`. The reference program is written for one: setup_inputs(seed, part) draws one part's arguments, and reference() takes and returns one part's arrays. A program takes and returns all parts, laid end to end along the dimension named above; each array names one. Nothing has to cross between parts.
Inputs may be any that keep to these rules, and one draw needn't show every extreme that they name: `mig_bit`: an entry b >= 0 pairs device i with device i XOR 2 ** b, whose entry is also b; -1 means the device has no partner. `send_table`: each source's 16 * 1 entries name each of its 8 blocks exactly once; the other entries are -1. `arr_index`: the first arr_count[o] entries of owner o name distinct slots s + c into which source s sends a block for o; later entries are 0. `arr_count`: the counts sum to 128.
All inputs are finite; a program needn't handle non-finite values.
Results may differ from the reference program's by a relative error of at most 0.0033.
Values may be sent and summed in bfloat16 or wider, within the bound.
No kernel may reach another device: no remote copies, remote signals or barrier semaphores. Data moves between devices by JAX's collectives and lax.ppermute only.
A program may use at most 128 MiB of HBM per device.

```python
import jax
import jax.numpy as jnp
from jax import lax

H = 128
DL = 512
DR = 64
BLK = 128
STEPS = 4
RB = 8
MB = 12
REQ = 1
OUTB = 8
RESB = 8
CAP = 1
ARRB = 15
LOGDP = 4
N_DP = 16


def load_factor(key):
    return jax.random.randint(jax.random.fold_in(key, 5), (N_DP,), 1, 5)


def skewed_lengths(key, salt, per_device, longest):
    factor = load_factor(key)
    drawn = jax.random.randint(jax.random.fold_in(key, salt), (N_DP, per_device), 1, longest + 1)
    lengths = jnp.maximum(1, drawn * factor[:, None] // 4).reshape(-1)
    forced = jax.random.randint(jax.random.fold_in(key, salt + 1), (), 0, N_DP * per_device)
    return jnp.where(jnp.arange(N_DP * per_device) == forced, longest, lengths).astype(jnp.int32)


def draw_res_len(key, part):
    return skewed_lengths(key, 6, REQ, RB * BLK)


def draw_mig_len(key, part):
    return skewed_lengths(key, 8, 1, MB * BLK)


def arrival_plan(key):
    seeded = jax.random.fold_in(key, 11)
    half_count = N_DP // 2
    spread = jax.random.randint(jax.random.fold_in(seeded, 1), (half_count,), 0, OUTB)
    forced = jax.random.randint(jax.random.fold_in(seeded, 2), (), 0, half_count)
    spread = jnp.where(jnp.arange(half_count) == forced, OUTB - 1, spread)
    counts = jnp.concatenate([OUTB + spread, OUTB - spread]).astype(jnp.int32)
    owner_order = jax.random.permutation(jax.random.fold_in(seeded, 3), N_DP).astype(jnp.int32)
    starts = jnp.cumsum(counts) - counts
    positions = jnp.arange(N_DP * OUTB, dtype=jnp.int32)
    segment = jnp.sum((starts[None, :] <= positions[:, None]).astype(jnp.int32), axis=1) - 1
    owners = owner_order[segment]
    within = positions - starts[segment]
    source = positions % N_DP
    pair_slot = within // N_DP
    row_keys = jax.random.split(jax.random.fold_in(seeded, 4), N_DP)
    shuffles = jax.vmap(lambda row_key: jax.random.permutation(row_key, OUTB))(row_keys).astype(jnp.int32)
    blocks = shuffles[source, positions // N_DP]
    send_rows = jnp.full((N_DP, N_DP * CAP), -1, jnp.int32).at[source, owners * CAP + pair_slot].set(blocks)
    listed = jnp.zeros((N_DP, ARRB), jnp.int32).at[owners, within].set(source * CAP + pair_slot)
    totals = jnp.zeros((N_DP,), jnp.int32).at[owner_order].set(counts)
    return (send_rows.reshape(-1), listed.reshape(-1), totals)


def draw_send_table(key, part):
    return arrival_plan(key)[0]


def draw_arr_index(key, part):
    return arrival_plan(key)[1]


def draw_arr_count(key, part):
    return arrival_plan(key)[2]


def draw_mig_bit(key, part):
    scores = jax.random.randint(jax.random.fold_in(key, 23), (N_DP, LOGDP), 1, 1 << 20)
    levels = jnp.arange(LOGDP, dtype=jnp.int32)

    def visit_device(device, chosen_bits):
        partners = jnp.bitwise_xor(device, jnp.left_shift(jnp.int32(1), levels))
        unpaired = (chosen_bits[partners] < 0) & (chosen_bits[device] < 0)
        ranking = jnp.where(unpaired, scores[device], 0)
        ranking = jnp.where((device == 0) & (levels == LOGDP - 1), 1 << 21, ranking)
        best_bit = jnp.argmax(ranking).astype(jnp.int32)
        chosen = jnp.max(ranking) > 0
        updated = chosen_bits.at[device].set(best_bit).at[partners[best_bit]].set(best_bit)
        return jnp.where(chosen, updated, chosen_bits)
    return lax.fori_loop(0, N_DP, visit_device, jnp.full((N_DP,), -1, jnp.int32))


def query_parts(key):
    seeded = jax.random.fold_in(key, 31)
    row_count = N_DP * (REQ + 2)
    fresh = jnp.clip(jax.random.normal(jax.random.fold_in(seeded, 4), (row_count, STEPS, DL + DR), jnp.float32), -6.0, 6.0)
    queries = jnp.clip(jax.random.normal(jax.random.fold_in(seeded, 5), (row_count, STEPS, H, DL), jnp.float32), -6.0, 6.0)
    return (fresh, queries)


def draw_q_lat(key, part):
    return query_parts(key)[1].astype(jnp.bfloat16)


def draw_new_kv(key, part):
    return query_parts(key)[0].astype(jnp.bfloat16)


def place_ends(values, own_key, smallest, high):
    index_at = [jax.random.randint(jax.random.fold_in(own_key, axis), (), 0, length) for axis, length in enumerate(values.shape)]
    main_axis = values.shape.index(max(values.shape))
    beside = index_at[:main_axis] + [(index_at[main_axis] + 1) % values.shape[main_axis]] + index_at[main_axis + 1:]
    return values.at[tuple(index_at)].set(smallest).at[tuple(beside)].set(high)


def block_levels(own_key, dims, cuts, least, high):
    loudness = 1.0
    for position, parts in cuts:
        heights = jax.random.uniform(jax.random.fold_in(jax.random.fold_in(own_key, 6), position), (parts,), jnp.float32, least / len(cuts), high / len(cuts))
        loudness = loudness * jnp.repeat(jnp.exp(heights), dims[position] // parts).reshape((-1,) + (1,) * (len(dims) - 1 - position))
    return loudness


def noise(own_key, shape, scale, most, cuts=(), held_as=jnp.bfloat16):
    factor_of = block_levels(own_key, shape, cuts, -0.22, 0.18) if cuts else 1.0
    values = jax.random.normal(own_key, shape, jnp.float32) * scale * factor_of
    return jnp.minimum(jnp.maximum(values, -most), most).astype(held_as)


def setup_inputs(seed: int = 0, part: int = 0) -> dict:
    key_of = jax.random.split(jax.random.key(seed), 18)
    own_keys = jax.random.split(jax.random.fold_in(key_of[17], part), 18)
    res_lat = noise(own_keys[0], (N_DP * RESB, BLK, DL), 1.0, 6.0, ((0, 16),))
    res_rope = noise(own_keys[1], (N_DP * RESB, DR, BLK), 1.0, 6.0, ((0, 16),))
    res_table = jax.vmap(lambda own: jax.random.permutation(own, RESB))(jax.random.split(own_keys[2], N_DP)).reshape((N_DP, RESB)).astype(jnp.int32)
    res_len = draw_res_len(jax.random.fold_in(jax.random.fold_in(key_of[17], part), 71), part)
    out_lat = noise(own_keys[4], (N_DP * OUTB, BLK, DL), 1.0, 6.0, ((0, 16),))
    out_rope = noise(own_keys[5], (N_DP * OUTB, DR, BLK), 1.0, 6.0, ((0, 16),))
    out_fill = place_ends(jax.random.randint(own_keys[6], (N_DP * OUTB,), 1, BLK + 1), jax.random.fold_in(own_keys[6], 1), 1, BLK).astype(jnp.int32)
    send_table = draw_send_table(jax.random.fold_in(jax.random.fold_in(key_of[17], part), 71), part)
    arr_index = draw_arr_index(jax.random.fold_in(jax.random.fold_in(key_of[17], part), 71), part)
    arr_count = draw_arr_count(jax.random.fold_in(jax.random.fold_in(key_of[17], part), 71), part)
    mig_lat = noise(own_keys[10], (N_DP * MB, BLK, DL), 1.0, 6.0, ((0, 16),))
    mig_rope = noise(own_keys[11], (N_DP * MB, DR, BLK), 1.0, 6.0, ((0, 16),))
    mig_len = draw_mig_len(jax.random.fold_in(jax.random.fold_in(key_of[17], part), 71), part)
    mig_bit = draw_mig_bit(jax.random.fold_in(jax.random.fold_in(key_of[17], part), 71), part)
    q_lat = draw_q_lat(jax.random.fold_in(jax.random.fold_in(key_of[17], part), 71), part)
    q_rope = noise(own_keys[15], (N_DP * (REQ + 2), STEPS, DR, H), 1.0, 6.0, ((0, 16),))
    new_kv = draw_new_kv(jax.random.fold_in(jax.random.fold_in(key_of[17], part), 71), part)
    return dict(res_lat=res_lat, res_rope=res_rope, res_table=res_table, res_len=res_len, out_lat=out_lat, out_rope=out_rope, out_fill=out_fill, send_table=send_table, arr_index=arr_index, arr_count=arr_count, mig_lat=mig_lat, mig_rope=mig_rope, mig_len=mig_len, mig_bit=mig_bit, q_lat=q_lat, q_rope=q_rope, new_kv=new_kv)


score_scale = 192.0 ** -0.5


def attend(q_lat, q_rope, new_kv, key_blocks, rope_blocks, usable):
    latent = key_blocks.shape[2]
    new_lat = new_kv[:, :latent].astype(jnp.float32)
    new_rope = new_kv[:, latent:].astype(jnp.float32)
    query_lat = q_lat.astype(jnp.float32)
    query_rope = q_rope.astype(jnp.float32)
    key_lat = key_blocks.astype(jnp.float32)
    cache_scores = (jnp.einsum("thd,nkd->thnk", query_lat, key_lat)
                    + jnp.einsum("tdh,ndk->thnk", query_rope, rope_blocks.astype(jnp.float32))) * score_scale
    cache_scores = jnp.where(usable[None, None], cache_scores, -jnp.inf)
    new_scores = (jnp.einsum("thd,ud->thu", query_lat, new_lat)
                  + jnp.einsum("tdh,ud->thu", query_rope, new_rope)) * score_scale
    step_count = new_kv.shape[0]
    causal = jnp.arange(step_count)[None, :] <= jnp.arange(step_count)[:, None]
    new_scores = jnp.where(causal[:, None, :], new_scores, -jnp.inf)
    highest = jnp.maximum(jnp.max(cache_scores, axis=(2, 3)), jnp.max(new_scores, axis=2))
    cache_w = jnp.exp(cache_scores - highest[:, :, None, None])
    new_w = jnp.exp(new_scores - highest[:, :, None])
    weight_sum = jnp.sum(cache_w, axis=(2, 3)) + jnp.sum(new_w, axis=2)
    cache_round = lax.optimization_barrier(cache_w.astype(jnp.bfloat16)).astype(jnp.float32)
    new_round = lax.optimization_barrier(new_w.astype(jnp.bfloat16)).astype(jnp.float32)
    combined = jnp.einsum("thnk,nkd->thd", cache_round, key_lat) + jnp.einsum("thu,ud->thd", new_round, new_lat)
    return (combined / weight_sum[:, :, None]).astype(jnp.bfloat16)


def reference(res_lat, res_rope, res_table, res_len, out_lat, out_rope, out_fill, send_table, arr_index, arr_count,
              mig_lat, mig_rope, mig_len, mig_bit, q_lat, q_rope, new_kv):
    slots = REQ + 2
    query_lat = q_lat.reshape(N_DP, slots, STEPS, H, DL)
    query_rope = q_rope.reshape(N_DP, slots, STEPS, DR, H)
    fresh_keys = new_kv.reshape(N_DP, slots, STEPS, DL + DR)
    res_lat_dev = res_lat.reshape(N_DP, RESB, BLK, DL)
    res_rope_dev = res_rope.reshape(N_DP, RESB, DR, BLK)
    tables = res_table.reshape(N_DP, REQ, RB)
    lengths = res_len.reshape(N_DP, REQ)
    out_lat_dev = out_lat.reshape(N_DP, OUTB, BLK, DL)
    out_rope_dev = out_rope.reshape(N_DP, OUTB, DR, BLK)
    fills = out_fill.reshape(N_DP, OUTB)
    sends = send_table.reshape(N_DP, N_DP * CAP)
    arrivals = arr_index.reshape(N_DP, ARRB)
    mig_lat_dev = mig_lat.reshape(N_DP, MB, BLK, DL)
    mig_rope_dev = mig_rope.reshape(N_DP, MB, DR, BLK)
    token_pos = jnp.arange(BLK, dtype=jnp.int32)

    def one_device(device):
        def resident(request):
            indices = tables[device, request]
            usable = (jnp.arange(RB * BLK, dtype=jnp.int32) < lengths[device, request]).reshape(RB, BLK)
            return attend(query_lat[device, request], query_rope[device, request], fresh_keys[device, request],
                          res_lat_dev[device][indices], res_rope_dev[device][indices], usable)

        resident_out = lax.map(resident, jnp.arange(REQ, dtype=jnp.int32))
        received = arrivals[device]
        source = received // CAP
        blocks = jnp.maximum(sends[source, device * CAP + received % CAP], 0)
        block_fill = fills[source, blocks]
        usable = (jnp.arange(ARRB, dtype=jnp.int32) < arr_count[device])[:, None] & (token_pos[None, :] < block_fill[:, None])
        arrival_out = attend(query_lat[device, REQ], query_rope[device, REQ], fresh_keys[device, REQ],
                             out_lat_dev[source, blocks], out_rope_dev[source, blocks], usable)
        partner_bit = mig_bit[device]
        partner = jnp.where(partner_bit >= 0,
                            jnp.bitwise_xor(device, jnp.left_shift(jnp.int32(1), jnp.maximum(partner_bit, 0))),
                            device).astype(jnp.int32)
        usable = (jnp.arange(MB * BLK, dtype=jnp.int32) < mig_len[partner]).reshape(MB, BLK)
        moved_out = attend(query_lat[device, REQ + 1], query_rope[device, REQ + 1], fresh_keys[device, REQ + 1],
                           mig_lat_dev[partner], mig_rope_dev[partner], usable)
        return jnp.concatenate([resident_out, arrival_out[None], moved_out[None]], axis=0)

    result = lax.map(one_device, jnp.arange(N_DP, dtype=jnp.int32))
    return result.reshape(N_DP * slots, STEPS, H, DL)
```

```python
import functools

import jax
import jax.numpy as jnp
from jax import lax
from jax.experimental import pallas as pl
from jax.experimental.pallas import tpu as pltpu
from jax.sharding import PartitionSpec as P

SCALE = 192.0 ** (-0.5)
MARK = 1e30
LIMIT = 1e20
ANY = pl.BlockSpec(memory_space=pl.ANY)
SMEM = pl.BlockSpec(memory_space=pltpu.SMEM)
DMA = pltpu.SemaphoreType.DMA


def contract_last(a, b):
    return lax.dot_general(a, b, (((1,), (1,)), ((), ())), preferred_element_type=jnp.float32)


def ceil_div(a, b):
    return (a + b - 1) // b


class Plan:
    def __init__(self, most, steps, heads, latent, rope, block):
        self.most = most + most % 2
        self.steps, self.heads, self.latent, self.rope, self.block = steps, heads, latent, rope, block
        self.rows = steps * heads
        self.pair = 2 * block

    def scratch(self):
        chunks = self.most // 2
        return [
            pltpu.VMEM((self.rows, self.latent), jnp.bfloat16),
            pltpu.VMEM((self.steps, self.rope, self.heads), jnp.bfloat16),
            pltpu.VMEM((self.rows, self.rope), jnp.bfloat16),
            pltpu.VMEM((self.steps, self.latent + self.rope), jnp.bfloat16),
            pltpu.VMEM((self.block, self.latent + self.rope), jnp.float32),
            pltpu.VMEM((chunks, self.pair, self.latent), jnp.bfloat16),
            pltpu.VMEM((chunks, self.rope, self.pair), jnp.bfloat16),
            pltpu.VMEM((chunks, self.rows, self.pair), jnp.float32),
            pltpu.VMEM((self.rows, self.pair), jnp.float32),
            pltpu.VMEM((self.rows, self.latent), jnp.float32),
            pltpu.VMEM((self.rows, self.latent), jnp.bfloat16),
            DMA((self.steps + 3,)),
            DMA((self.most,)),
            DMA((self.most, 4)),
        ]


def attention(plan, scr, q_lat, q_rope, fresh, block_copies, count, limit, marked, out_copy):
    (qbuf, qrbuf, qrt, newraw, newpad, kbuf, rbuf, sbuf, mbuf, acc, obuf, qsem, ksem, rsem) = scr
    steps, heads, latent, pair = plan.steps, plan.heads, plan.latent, plan.pair
    copies = [
        pltpu.make_async_copy(q_lat.at[t], qbuf.at[pl.ds(t * heads, heads)], qsem.at[t])
        for t in range(steps)
    ]
    copies.append(pltpu.make_async_copy(q_rope, qrbuf, qsem.at[steps]))
    copies.append(pltpu.make_async_copy(fresh, newraw, qsem.at[steps + 1]))
    for copy in copies:
        copy.start()
    chunks = ceil_div(count, 2)

    def each(j, what):
        for copy in block_copies(jnp.minimum(j, count - 1), j, kbuf, rbuf, ksem, rsem):
            what(copy)

    def launch(j, carry):
        each(j, lambda copy: copy.start())
        return carry

    lax.fori_loop(0, 2 * chunks, launch, 0)
    for copy in copies:
        copy.wait()
    for t in range(steps):
        qrt[pl.ds(t * heads, heads), :] = qrbuf[t].astype(jnp.float32).T.astype(jnp.bfloat16)
    newpad[...] = jnp.zeros_like(newpad)
    newpad[0:steps, :] = newraw[...].astype(jnp.float32)
    new_lat = newpad[:, :latent].astype(jnp.bfloat16)
    new_rope = newpad[:, latent:].astype(jnp.bfloat16)
    fresh_scores = (contract_last(qbuf[...], new_lat) + contract_last(qrt[...], new_rope)) * SCALE
    step_of = lax.broadcasted_iota(jnp.int32, (plan.rows, plan.block), 0) // heads
    new_of = lax.broadcasted_iota(jnp.int32, (plan.rows, plan.block), 1)
    fresh_scores = jnp.where(new_of <= step_of, fresh_scores, -jnp.inf)
    mbuf[...] = jnp.full_like(mbuf, -jnp.inf)

    def score(c, carry):
        each(2 * c, lambda copy: copy.wait())
        each(2 * c + 1, lambda copy: copy.wait())
        rope = rbuf[c]
        s = contract_last(qbuf[...], kbuf[c]) + jnp.dot(
            qrt[...], rope, preferred_element_type=jnp.float32
        )
        usable = lax.broadcasted_iota(jnp.int32, (1, pair), 1) + c * pair < limit
        if marked:
            usable = usable & (rope[0:1, :].astype(jnp.float32) < LIMIT)
        s = jnp.where(usable, s * SCALE, -jnp.inf)
        sbuf[c] = s
        mbuf[...] = jnp.maximum(mbuf[...], s)
        return carry

    lax.fori_loop(0, chunks, score, 0)
    highest = jnp.maximum(
        jnp.max(mbuf[...], axis=1, keepdims=True), jnp.max(fresh_scores, axis=1, keepdims=True)
    )
    new_w = jnp.exp(fresh_scores - highest)
    new_sum = jnp.sum(new_w, axis=1, keepdims=True)
    acc[...] = jnp.dot(new_w.astype(jnp.bfloat16), new_lat, preferred_element_type=jnp.float32)
    mbuf[...] = jnp.zeros_like(mbuf)

    def weigh(c, carry):
        w = jnp.exp(sbuf[c] - highest)
        mbuf[...] += w
        acc[...] += jnp.dot(w.astype(jnp.bfloat16), kbuf[c], preferred_element_type=jnp.float32)
        return carry

    lax.fori_loop(0, chunks, weigh, 0)
    total = new_sum + jnp.sum(mbuf[...], axis=1, keepdims=True)
    obuf[...] = (acc[...] / total).astype(jnp.bfloat16)
    outs = [out_copy(t, obuf.at[pl.ds(t * heads, heads)], qsem.at[t]) for t in range(steps)]
    for copy in outs:
        copy.start()
    for copy in outs:
        copy.wait()


def plain_copies(lat, rope, pick, block):
    def copies(source, j, kbuf, rbuf, ksem, rsem):
        b = pick(source)
        c, side = j // 2, pl.multiple_of((j % 2) * block, block)
        return [
            pltpu.make_async_copy(lat.at[b], kbuf.at[c, pl.ds(side, block)], ksem.at[j]),
            pltpu.make_async_copy(rope.at[b], rbuf.at[c, :, pl.ds(side, block)], rsem.at[j, 0]),
        ]

    return copies


def packed_copies(got, pick, block, rope_rows, latent):
    parts = latent // block

    def copies(source, j, kbuf, rbuf, ksem, rsem):
        e = pick(source)
        c, side = j // 2, pl.multiple_of((j % 2) * block, block)
        out = [
            pltpu.make_async_copy(
                got.at[e, pl.ds(0, block)], kbuf.at[c, pl.ds(side, block)], ksem.at[j]
            )
        ]
        for g in range(parts):
            out.append(
                pltpu.make_async_copy(
                    got.at[e, pl.ds(block, rope_rows), pl.ds(g * block, block)],
                    rbuf.at[c, pl.ds(g * rope_rows, rope_rows), pl.ds(side, block)],
                    rsem.at[j, g],
                )
            )
        return out

    return copies


def cost(plan):
    keys = plan.most * plan.block
    return pl.CostEstimate(
        flops=2 * plan.rows * keys * (2 * plan.latent + plan.rope) // 2,
        bytes_accessed=2 * keys * (plan.latent + plan.rope) // 2,
        transcendentals=plan.rows * keys // 2,
    )


def resident_kernel(plan, slot, table, length, q_lat, q_rope, fresh, lat, rope, out, *scr):
    used = length[0]
    attention(
        plan, scr, q_lat.at[slot], q_rope.at[slot], fresh.at[slot],
        plain_copies(lat, rope, lambda j: table[0, j], plan.block),
        ceil_div(used, plan.block), used, False,
        lambda t, src, sem: pltpu.make_async_copy(src, out.at[slot, t], sem),
    )


def migrated_kernel(plan, slot, length, q_lat, q_rope, fresh, lat, rope, out, *scr):
    used = length[0]
    at = (lambda ref: ref) if slot is None else (lambda ref: ref.at[slot])
    attention(
        plan, scr, at(q_lat), at(q_rope), at(fresh),
        plain_copies(lat, rope, lambda j: j, plan.block),
        ceil_div(used, plan.block), used, False,
        lambda t, src, sem: pltpu.make_async_copy(src, out.at[t], sem),
    )


def arriving_kernel(plan, slot, index, arrived, q_lat, q_rope, fresh, got, moved, base, out, mbuf, msem, *scr):
    del base
    fetch = pltpu.make_async_copy(moved, mbuf, msem.at[0])
    fetch.start()
    used = arrived[0]

    def finish(t, src, sem):
        return pltpu.make_async_copy(src, out.at[slot, t], sem)

    fetch.wait()
    put = pltpu.make_async_copy(mbuf, out.at[slot + 1], msem.at[1])
    put.start()
    attention(
        plan, scr, q_lat.at[slot], q_rope.at[slot], fresh.at[slot],
        packed_copies(got, lambda j: index[j], plan.block, plan.rope * plan.block // plan.latent, plan.latent),
        used, used * plan.block, True, finish,
    )
    put.wait()


def pack_kernel(table, fill, lat, rope, out, lbuf, rbuf, pbuf, lsem, rsem, osem):
    blocks, block, latent = lat.shape
    rows = pbuf.shape[1]
    pulls = [pltpu.make_async_copy(lat.at[b], lbuf.at[b], lsem.at[b]) for b in range(blocks)]
    small = pltpu.make_async_copy(rope, rbuf, rsem)
    small.start()
    for pull in pulls:
        pull.start()
    small.wait()
    first = lax.broadcasted_iota(jnp.int32, rope.shape[1:], 0) == 0
    token = lax.broadcasted_iota(jnp.int32, rope.shape[1:], 1)
    for b in range(blocks):
        marked = jnp.where(first & (token >= fill[b]), MARK, rbuf[b].astype(jnp.float32)).astype(jnp.bfloat16)
        for g in range(latent // block):
            pbuf[b, :, g * block : (g + 1) * block] = marked[g * rows : (g + 1) * rows]
    for pull in pulls:
        pull.wait()

    def each(o, what):
        b = table[o]

        @pl.when(b >= 0)
        def _():
            for copy in (
                pltpu.make_async_copy(lbuf.at[b], out.at[o, pl.ds(0, block)], osem.at[b, 0]),
                pltpu.make_async_copy(pbuf.at[b], out.at[o, pl.ds(block, rows)], osem.at[b, 1]),
            ):
                what(copy)

    def launch(o, carry):
        each(o, lambda copy: copy.start())
        return carry

    def settle(o, carry):
        each(o, lambda copy: copy.wait())
        return carry

    lax.fori_loop(0, out.shape[0], launch, 0)
    lax.fori_loop(0, out.shape[0], settle, 0)


def shards(
    res_lat, res_rope, res_table, res_len, out_lat, out_rope, out_fill, send_table, arr_index,
    arr_count, mig_lat, mig_rope, mig_len, mig_bit, q_lat, q_rope, new_kv,
):
    count = lax.axis_size("dp")
    bits = count.bit_length() - 1
    slots, steps, heads, latent = q_lat.shape
    rope = q_rope.shape[2]
    block = res_lat.shape[1]
    requests = res_len.shape[0]
    assert requests == 1 and send_table.shape[0] == count
    make = functools.partial(Plan, steps=steps, heads=heads, latent=latent, rope=rope, block=block)
    rows = rope * block // latent
    blocks = out_lat.shape[0]

    packed = pl.pallas_call(
        pack_kernel,
        out_shape=jax.ShapeDtypeStruct((count, block + rows, latent), jnp.bfloat16),
        in_specs=[SMEM, SMEM, ANY, ANY],
        out_specs=ANY,
        scratch_shapes=[
            pltpu.VMEM((blocks, block, latent), jnp.bfloat16),
            pltpu.VMEM((blocks, rope, block), jnp.bfloat16),
            pltpu.VMEM((blocks, rows, latent), jnp.bfloat16),
            DMA((blocks,)), DMA, DMA((blocks, 2)),
        ],
        name="pack",
    )(send_table, out_fill, out_lat, out_rope)
    got = lax.all_to_all(packed, "dp", split_axis=0, concat_axis=0, tiled=True)

    plan = make(res_table.shape[1])
    base = pl.pallas_call(
        functools.partial(resident_kernel, plan, 0),
        out_shape=jax.ShapeDtypeStruct((slots, steps, heads, latent), jnp.bfloat16),
        in_specs=[SMEM, SMEM, ANY, ANY, ANY, ANY, ANY],
        out_specs=ANY,
        scratch_shapes=plan.scratch(),
        cost_estimate=cost(plan),
        name="resident",
    )(res_table, res_len, q_lat, q_rope, new_kv, res_lat, res_rope)

    moved_slot = requests + 1

    def migrated(length, query, query_rope, fresh, lat, rot, slot):
        plan = make(lat.shape[0])
        return pl.pallas_call(
            functools.partial(migrated_kernel, plan, slot),
            out_shape=jax.ShapeDtypeStruct((steps, heads, latent), jnp.bfloat16),
            in_specs=[SMEM, ANY, ANY, ANY, ANY, ANY],
            out_specs=ANY,
            scratch_shapes=plan.scratch(),
            cost_estimate=cost(plan),
            name="migrated",
        )(length, query, query_rope, fresh, lat, rot)

    def stay(length, q_lat, q_rope, new_kv, lat, rot):
        return migrated(length, q_lat, q_rope, new_kv, lat, rot, moved_slot)

    def with_partner(bit):
        route = [(i, i ^ 1 << bit) for i in range(count)]

        def swap(x):
            return lax.ppermute(x, "dp", route)

        def branch(length, q_lat, q_rope, new_kv, lat, rot):
            visitor = [swap(x[moved_slot]) for x in (q_lat, q_rope, new_kv)]
            return swap(migrated(length, *visitor, lat, rot, None))

        return branch

    moved = lax.switch(
        mig_bit[0] + 1,
        [stay] + [with_partner(bit) for bit in range(bits)],
        mig_len, q_lat, q_rope, new_kv, mig_lat, mig_rope,
    )

    plan = make(arr_index.shape[0])
    return pl.pallas_call(
        functools.partial(arriving_kernel, plan, requests),
        out_shape=jax.ShapeDtypeStruct((slots, steps, heads, latent), jnp.bfloat16),
        in_specs=[SMEM, SMEM, ANY, ANY, ANY, ANY, ANY, ANY],
        out_specs=ANY,
        scratch_shapes=[pltpu.VMEM((steps, heads, latent), jnp.bfloat16), DMA((2,))] + plan.scratch(),
        input_output_aliases={7: 0},
        cost_estimate=cost(plan),
        name="arriving",
    )(arr_index, arr_count, q_lat, q_rope, new_kv, got, moved, base)


def solution(mesh):
    whole = P(("groups", "dp"))
    return jax.shard_map(shards, mesh=mesh, in_specs=(whole,) * 17, out_specs=whole, check_vma=False)
```

```python
import functools

import jax
import jax.numpy as jnp
from jax import lax
from jax.experimental import pallas as pl
from jax.experimental.pallas import tpu as pltpu
from jax.sharding import PartitionSpec as P

SCALE = 192.0 ** (-0.5)
MARK = 1e30
LIMIT = 1e20
ANY = pl.BlockSpec(memory_space=pl.ANY)
SMEM = pl.BlockSpec(memory_space=pltpu.SMEM)
DMA = pltpu.SemaphoreType.DMA


def contract_last(a, b):
    return lax.dot_general(a, b, (((1,), (1,)), ((), ())), preferred_element_type=jnp.float32)


def ceil_div(a, b):
    return (a + b - 1) // b


class Plan:
    def __init__(self, most, steps, heads, latent, rope, block):
        self.most = most + most % 2
        self.steps, self.heads, self.latent, self.rope, self.block = steps, heads, latent, rope, block
        self.rows = steps * heads
        self.pair = 2 * block

    def scratch(self):
        chunks = self.most // 2
        return [
            pltpu.VMEM((self.rows, self.latent), jnp.bfloat16),
            pltpu.VMEM((self.steps, self.rope, self.heads), jnp.bfloat16),
            pltpu.VMEM((self.rows, self.rope), jnp.bfloat16),
            pltpu.VMEM((self.steps, self.latent + self.rope), jnp.bfloat16),
            pltpu.VMEM((self.block, self.latent + self.rope), jnp.float32),
            pltpu.VMEM((chunks, self.pair, self.latent), jnp.bfloat16),
            pltpu.VMEM((chunks, self.rope, self.pair), jnp.bfloat16),
            pltpu.VMEM((chunks, self.rows, self.pair), jnp.float32),
            pltpu.VMEM((self.rows, self.pair), jnp.float32),
            pltpu.VMEM((self.rows, self.latent), jnp.float32),
            pltpu.VMEM((self.rows, self.latent), jnp.bfloat16),
            DMA((self.steps + 3,)),
            DMA((self.most,)),
            DMA((self.most, 4)),
        ]


def attention(plan, scr, q_lat, q_rope, fresh, block_copies, count, limit, marked, out_copy):
    (qbuf, qrbuf, qrt, newraw, newpad, kbuf, rbuf, sbuf, mbuf, acc, obuf, qsem, ksem, rsem) = scr
    steps, heads, latent, pair = plan.steps, plan.heads, plan.latent, plan.pair
    copies = [
        pltpu.make_async_copy(q_lat.at[t], qbuf.at[pl.ds(t * heads, heads)], qsem.at[t])
        for t in range(steps)
    ]
    copies.append(pltpu.make_async_copy(q_rope, qrbuf, qsem.at[steps]))
    copies.append(pltpu.make_async_copy(fresh, newraw, qsem.at[steps + 1]))
    for copy in copies:
        copy.start()
    chunks = ceil_div(count, 2)

    def each(j, what):
        block_copies(j, jnp.minimum(j, count - 1), what, kbuf, rbuf, ksem, rsem)

    def launch(j, carry):
        each(j, lambda copy: copy.start())
        return carry

    lax.fori_loop(0, 2 * chunks, launch, 0)
    for copy in copies:
        copy.wait()
    for t in range(steps):
        qrt[pl.ds(t * heads, heads), :] = qrbuf[t].astype(jnp.float32).T.astype(jnp.bfloat16)
    newpad[...] = jnp.zeros_like(newpad)
    newpad[0:steps, :] = newraw[...].astype(jnp.float32)
    new_lat = newpad[:, :latent].astype(jnp.bfloat16)
    new_rope = newpad[:, latent:].astype(jnp.bfloat16)
    fresh_scores = (contract_last(qbuf[...], new_lat) + contract_last(qrt[...], new_rope)) * SCALE
    step_of = lax.broadcasted_iota(jnp.int32, (plan.rows, plan.block), 0) // heads
    new_of = lax.broadcasted_iota(jnp.int32, (plan.rows, plan.block), 1)
    fresh_scores = jnp.where(new_of <= step_of, fresh_scores, -jnp.inf)
    mbuf[...] = jnp.full_like(mbuf, -jnp.inf)

    def score(c, carry):
        each(2 * c, lambda copy: copy.wait())
        each(2 * c + 1, lambda copy: copy.wait())
        rope = rbuf[c]
        s = contract_last(qbuf[...], kbuf[c]) + jnp.dot(
            qrt[...], rope, preferred_element_type=jnp.float32
        )
        usable = lax.broadcasted_iota(jnp.int32, (1, pair), 1) + c * pair < limit
        if marked:
            usable = usable & (rope[0:1, :].astype(jnp.float32) < LIMIT)
        s = jnp.where(usable, s * SCALE, -jnp.inf)
        sbuf[c] = s
        mbuf[...] = jnp.maximum(mbuf[...], s)
        return carry

    lax.fori_loop(0, chunks, score, 0)
    highest = jnp.maximum(
        jnp.max(mbuf[...], axis=1, keepdims=True), jnp.max(fresh_scores, axis=1, keepdims=True)
    )
    new_w = jnp.exp(fresh_scores - highest)
    new_sum = jnp.sum(new_w, axis=1, keepdims=True)
    acc[...] = jnp.dot(new_w.astype(jnp.bfloat16), new_lat, preferred_element_type=jnp.float32)
    mbuf[...] = jnp.zeros_like(mbuf)

    def weigh(c, carry):
        w = jnp.exp(sbuf[c] - highest)
        mbuf[...] += w
        acc[...] += jnp.dot(w.astype(jnp.bfloat16), kbuf[c], preferred_element_type=jnp.float32)
        return carry

    lax.fori_loop(0, chunks, weigh, 0)
    total = new_sum + jnp.sum(mbuf[...], axis=1, keepdims=True)
    obuf[...] = (acc[...] / total).astype(jnp.bfloat16)
    outs = [out_copy(t, obuf.at[pl.ds(t * heads, heads)], qsem.at[t]) for t in range(steps)]
    for copy in outs:
        copy.start()
    for copy in outs:
        copy.wait()


def plain_copies(lat, rope, pick, block):
    def copies(source, j, kbuf, rbuf, ksem, rsem):
        b = pick(source)
        c, side = j // 2, pl.multiple_of((j % 2) * block, block)
        return [
            pltpu.make_async_copy(lat.at[b], kbuf.at[c, pl.ds(side, block)], ksem.at[j]),
            pltpu.make_async_copy(rope.at[b], rbuf.at[c, :, pl.ds(side, block)], rsem.at[j, 0]),
        ]

    return copies


def every(copies):
    def each(j, source, what, *bufs):
        for copy in copies(source, j, *bufs):
            what(copy)

    return each


def packed_copies(got, pick, block, rope_rows, latent):
    parts = latent // block

    def copies(source, j, kbuf, rbuf, ksem, rsem):
        e = pick(source)
        c, side = j // 2, pl.multiple_of((j % 2) * block, block)
        out = [
            pltpu.make_async_copy(
                got.at[e, pl.ds(0, block)], kbuf.at[c, pl.ds(side, block)], ksem.at[j]
            )
        ]
        for g in range(parts):
            out.append(
                pltpu.make_async_copy(
                    got.at[e, pl.ds(block, rope_rows), pl.ds(g * block, block)],
                    rbuf.at[c, pl.ds(g * rope_rows, rope_rows), pl.ds(side, block)],
                    rsem.at[j, g],
                )
            )
        return out

    return copies


def chunk_spans(blocks):
    sizes = []
    while blocks > 0:
        sizes.append(min(3 if not sizes or blocks == 3 else 2, blocks))
        blocks -= sizes[-1]
    return sizes


def cost(plan):
    keys = plan.most * plan.block
    return pl.CostEstimate(
        flops=2 * plan.rows * keys * (2 * plan.latent + plan.rope) // 2,
        bytes_accessed=2 * keys * (plan.latent + plan.rope) // 2,
        transcendentals=plan.rows * keys // 2,
    )


def resident_kernel(plan, slot, table, length, q_lat, q_rope, fresh, lat, rope, out, *scr):
    used = length[0]
    attention(
        plan, scr, q_lat.at[slot], q_rope.at[slot], fresh.at[slot],
        every(plain_copies(lat, rope, lambda j: table[0, j], plan.block)),
        ceil_div(used, plan.block), used, False,
        lambda t, src, sem: pltpu.make_async_copy(src, out.at[slot, t], sem),
    )


def migrated_kernel(plan, slot, sizes, length, q_lat, q_rope, fresh, *refs):
    chunks, out, scr = refs[: len(sizes)], refs[len(sizes)], refs[len(sizes) + 1 :]
    used = length[0]
    rope_rows = plan.rope * plan.block // plan.latent
    starts = [sum(sizes[:i]) for i in range(len(sizes))]

    def each(j, source, what, kbuf, rbuf, ksem, rsem):
        for ref, first, size in zip(chunks, starts, sizes, strict=True):

            @pl.when((source >= first) & (source < first + size))
            def _(ref=ref, first=first):
                for copy in packed_copies(ref, lambda e: e - first, plan.block, rope_rows, plan.latent)(
                    source, j, kbuf, rbuf, ksem, rsem
                ):
                    what(copy)

    attention(
        plan, scr, q_lat.at[slot], q_rope.at[slot], fresh.at[slot], each,
        ceil_div(used, plan.block), used, False,
        lambda t, src, sem: pltpu.make_async_copy(src, out.at[t], sem),
    )


def arriving_kernel(plan, slot, index, arrived, q_lat, q_rope, fresh, got, moved, base, out, mbuf, msem, *scr):
    del base
    fetch = pltpu.make_async_copy(moved, mbuf, msem.at[0])
    fetch.start()
    used = arrived[0]

    def finish(t, src, sem):
        return pltpu.make_async_copy(src, out.at[slot, t], sem)

    fetch.wait()
    put = pltpu.make_async_copy(mbuf, out.at[slot + 1], msem.at[1])
    put.start()
    attention(
        plan, scr, q_lat.at[slot], q_rope.at[slot], fresh.at[slot],
        every(packed_copies(got, lambda j: index[j], plan.block, plan.rope * plan.block // plan.latent, plan.latent)),
        used, used * plan.block, True, finish,
    )
    put.wait()


def pack_rope(rope, rows, latent, block, put):
    for g in range(latent // block):
        put(g * block, rope[g * rows : (g + 1) * rows])


def pack_kernel(sizes, table, fill, lat, rope, mig_lat, mig_rope, *refs):
    out, moves = refs[0], refs[1 : 1 + len(sizes)]
    lbuf, rbuf, pbuf, mlbuf, mrbuf, mpbuf, lsem, msem, rsem, osem, csem = refs[1 + len(sizes) :]
    blocks, block, latent = lat.shape
    rows = pbuf.shape[1]
    small = [pltpu.make_async_copy(rope, rbuf, rsem.at[0]), pltpu.make_async_copy(mig_rope, mrbuf, rsem.at[1])]
    pulls = [pltpu.make_async_copy(lat.at[b], lbuf.at[b], lsem.at[b]) for b in range(blocks)]
    mpulls = [pltpu.make_async_copy(mig_lat.at[b], mlbuf.at[b], msem.at[b]) for b in range(mig_lat.shape[0])]
    for copy in small + mpulls + pulls:
        copy.start()
    for copy in small:
        copy.wait()
    for b in range(mig_lat.shape[0]):
        for g in range(latent // block):
            mpbuf[b, :, g * block : (g + 1) * block] = mrbuf[b, g * rows : (g + 1) * rows]
    first = lax.broadcasted_iota(jnp.int32, rope.shape[1:], 0) == 0
    token = lax.broadcasted_iota(jnp.int32, rope.shape[1:], 1)
    for b in range(blocks):
        marked = jnp.where(first & (token >= fill[b]), MARK, rbuf[b].astype(jnp.float32)).astype(jnp.bfloat16)
        for g in range(latent // block):
            pbuf[b, :, g * block : (g + 1) * block] = marked[g * rows : (g + 1) * rows]
    for copy in mpulls + pulls:
        copy.wait()
    done = []
    b = 0
    for ref, size in zip(moves, sizes, strict=True):
        for i in range(size):
            done.append(pltpu.make_async_copy(mlbuf.at[b], ref.at[i, pl.ds(0, block)], csem.at[b, 0]))
            done.append(pltpu.make_async_copy(mpbuf.at[b], ref.at[i, pl.ds(block, rows)], csem.at[b, 1]))
            b += 1
    for copy in done:
        copy.start()

    def each(o, what):
        b = table[o]

        @pl.when(b >= 0)
        def _():
            for copy in (
                pltpu.make_async_copy(lbuf.at[b], out.at[o, pl.ds(0, block)], osem.at[b, 0]),
                pltpu.make_async_copy(pbuf.at[b], out.at[o, pl.ds(block, rows)], osem.at[b, 1]),
            ):
                what(copy)

    def launch(o, carry):
        each(o, lambda copy: copy.start())
        return carry

    def settle(o, carry):
        each(o, lambda copy: copy.wait())
        return carry

    lax.fori_loop(0, out.shape[0], launch, 0)
    lax.fori_loop(0, out.shape[0], settle, 0)
    for copy in done:
        copy.wait()


def shards(
    res_lat, res_rope, res_table, res_len, out_lat, out_rope, out_fill, send_table, arr_index,
    arr_count, mig_lat, mig_rope, mig_len, mig_bit, q_lat, q_rope, new_kv,
):
    count = lax.axis_size("dp")
    bits = count.bit_length() - 1
    slots, steps, heads, latent = q_lat.shape
    rope = q_rope.shape[2]
    block = res_lat.shape[1]
    requests = res_len.shape[0]
    assert requests == 1 and send_table.shape[0] == count
    make = functools.partial(Plan, steps=steps, heads=heads, latent=latent, rope=rope, block=block)
    rows = rope * block // latent
    blocks = out_lat.shape[0]

    held = mig_lat.shape[0]
    sizes = chunk_spans(held)
    packed, *chunks = pl.pallas_call(
        functools.partial(pack_kernel, sizes),
        out_shape=[
            jax.ShapeDtypeStruct((n, block + rows, latent), jnp.bfloat16) for n in [count, *sizes]
        ],
        in_specs=[SMEM, SMEM, ANY, ANY, ANY, ANY],
        out_specs=[ANY] * (1 + len(sizes)),
        scratch_shapes=[
            pltpu.VMEM((blocks, block, latent), jnp.bfloat16),
            pltpu.VMEM((blocks, rope, block), jnp.bfloat16),
            pltpu.VMEM((blocks, rows, latent), jnp.bfloat16),
            pltpu.VMEM((held, block, latent), jnp.bfloat16),
            pltpu.VMEM((held, rope, block), jnp.bfloat16),
            pltpu.VMEM((held, rows, latent), jnp.bfloat16),
            DMA((blocks,)), DMA((held,)), DMA((2,)), DMA((blocks, 2)), DMA((held, 2)),
        ],
        name="pack",
    )(send_table, out_fill, out_lat, out_rope, mig_lat, mig_rope)

    ends = [sum(sizes[: i + 1]) * block for i in range(len(sizes))]

    def with_partner(bit):
        route = [(i, i ^ 1 << bit) for i in range(count)]

        def swap(x):
            return lax.ppermute(x, "dp", route)

        def branch(length, chunks):
            other = swap(length)
            longest = jnp.maximum(length, other)[0]
            level = sum((longest > end).astype(jnp.int32) for end in ends[:-1])

            def sending(k):
                return lambda chunks: [swap(x) if i <= k else x for i, x in enumerate(chunks)]

            return other, lax.switch(level, [sending(k) for k in range(len(sizes))], chunks)

        return branch

    length, chunks = lax.switch(
        mig_bit[0] + 1,
        [lambda length, chunks: (length, chunks)] + [with_partner(bit) for bit in range(bits)],
        mig_len, chunks,
    )
    packed, length, chunks = lax.optimization_barrier((packed, length, chunks))
    got = lax.all_to_all(packed, "dp", split_axis=0, concat_axis=0, tiled=True)

    plan = make(res_table.shape[1])
    base = pl.pallas_call(
        functools.partial(resident_kernel, plan, 0),
        out_shape=jax.ShapeDtypeStruct((slots, steps, heads, latent), jnp.bfloat16),
        in_specs=[SMEM, SMEM, ANY, ANY, ANY, ANY, ANY],
        out_specs=ANY,
        scratch_shapes=plan.scratch(),
        cost_estimate=cost(plan),
        name="resident",
    )(res_table, res_len, q_lat, q_rope, new_kv, res_lat, res_rope)

    plan = make(held)
    moved = pl.pallas_call(
        functools.partial(migrated_kernel, plan, requests + 1, sizes),
        out_shape=jax.ShapeDtypeStruct((steps, heads, latent), jnp.bfloat16),
        in_specs=[SMEM] + [ANY] * (3 + len(sizes)),
        out_specs=ANY,
        scratch_shapes=plan.scratch(),
        cost_estimate=cost(plan),
        name="migrated",
    )(length, q_lat, q_rope, new_kv, *chunks)

    plan = make(arr_index.shape[0])
    return pl.pallas_call(
        functools.partial(arriving_kernel, plan, requests),
        out_shape=jax.ShapeDtypeStruct((slots, steps, heads, latent), jnp.bfloat16),
        in_specs=[SMEM, SMEM, ANY, ANY, ANY, ANY, ANY, ANY],
        out_specs=ANY,
        scratch_shapes=[pltpu.VMEM((steps, heads, latent), jnp.bfloat16), DMA((2,))] + plan.scratch(),
        input_output_aliases={7: 0},
        cost_estimate=cost(plan),
        name="arriving",
    )(arr_index, arr_count, q_lat, q_rope, new_kv, got, moved, base)


def solution(mesh):
    whole = P(("groups", "dp"))
    return jax.shard_map(shards, mesh=mesh, in_specs=(whole,) * 17, out_specs=whole, check_vma=False)
```

```python
import functools

import jax
import jax.numpy as jnp
from jax import lax
from jax.experimental import pallas as pl
from jax.experimental.pallas import tpu as pltpu
from jax.sharding import PartitionSpec as P

SCALE = 192.0 ** (-0.5)
MARK = 1e30
LIMIT = 1e20
ANY = pl.BlockSpec(memory_space=pl.ANY)
SMEM = pl.BlockSpec(memory_space=pltpu.SMEM)
DMA = pltpu.SemaphoreType.DMA


def contract_last(a, b):
    return lax.dot_general(a, b, (((1,), (1,)), ((), ())), preferred_element_type=jnp.float32)


def ceil_div(a, b):
    return (a + b - 1) // b


class Plan:
    def __init__(self, most, steps, heads, latent, rope, block):
        self.most = most + most % 2
        self.steps, self.heads, self.latent, self.rope, self.block = steps, heads, latent, rope, block
        self.rows = steps * heads
        self.pair = 2 * block

    def scratch(self):
        chunks = self.most // 2
        return [
            pltpu.VMEM((self.rows, self.latent), jnp.bfloat16),
            pltpu.VMEM((self.steps, self.rope, self.heads), jnp.bfloat16),
            pltpu.VMEM((self.rows, self.rope), jnp.bfloat16),
            pltpu.VMEM((self.steps, self.latent + self.rope), jnp.bfloat16),
            pltpu.VMEM((self.block, self.latent + self.rope), jnp.float32),
            pltpu.VMEM((chunks, self.pair, self.latent), jnp.bfloat16),
            pltpu.VMEM((chunks, self.rope, self.pair), jnp.bfloat16),
            pltpu.VMEM((chunks, self.rows, self.pair), jnp.float32),
            pltpu.VMEM((self.rows, self.pair), jnp.float32),
            pltpu.VMEM((self.rows, self.latent), jnp.float32),
            pltpu.VMEM((self.rows, self.latent), jnp.bfloat16),
            DMA((self.steps + 3,)),
            DMA((self.most,)),
            DMA((self.most, 4)),
        ]


def attention(plan, scr, q_lat, q_rope, fresh, block_copies, count, limit, marked, out_copy):
    (qbuf, qrbuf, qrt, newraw, newpad, kbuf, rbuf, sbuf, mbuf, acc, obuf, qsem, ksem, rsem) = scr
    steps, heads, latent, pair = plan.steps, plan.heads, plan.latent, plan.pair
    copies = [
        pltpu.make_async_copy(q_lat.at[t], qbuf.at[pl.ds(t * heads, heads)], qsem.at[t])
        for t in range(steps)
    ]
    copies.append(pltpu.make_async_copy(q_rope, qrbuf, qsem.at[steps]))
    copies.append(pltpu.make_async_copy(fresh, newraw, qsem.at[steps + 1]))
    for copy in copies:
        copy.start()
    chunks = ceil_div(count, 2)

    def each(j, what):
        block_copies(j, jnp.minimum(j, count - 1), what, kbuf, rbuf, ksem, rsem)

    def launch(j, carry):
        each(j, lambda copy: copy.start())
        return carry

    lax.fori_loop(0, 2 * chunks, launch, 0)
    for copy in copies:
        copy.wait()
    for t in range(steps):
        qrt[pl.ds(t * heads, heads), :] = qrbuf[t].astype(jnp.float32).T.astype(jnp.bfloat16)
    newpad[...] = jnp.zeros_like(newpad)
    newpad[0:steps, :] = newraw[...].astype(jnp.float32)
    new_lat = newpad[:, :latent].astype(jnp.bfloat16)
    new_rope = newpad[:, latent:].astype(jnp.bfloat16)
    fresh_scores = (contract_last(qbuf[...], new_lat) + contract_last(qrt[...], new_rope)) * SCALE
    step_of = lax.broadcasted_iota(jnp.int32, (plan.rows, plan.block), 0) // heads
    new_of = lax.broadcasted_iota(jnp.int32, (plan.rows, plan.block), 1)
    fresh_scores = jnp.where(new_of <= step_of, fresh_scores, -jnp.inf)
    mbuf[...] = jnp.full_like(mbuf, -jnp.inf)

    def score(c, carry):
        each(2 * c, lambda copy: copy.wait())
        each(2 * c + 1, lambda copy: copy.wait())
        rope = rbuf[c]
        s = contract_last(qbuf[...], kbuf[c]) + jnp.dot(
            qrt[...], rope, preferred_element_type=jnp.float32
        )
        usable = lax.broadcasted_iota(jnp.int32, (1, pair), 1) + c * pair < limit
        if marked:
            usable = usable & (rope[0:1, :].astype(jnp.float32) < LIMIT)
        s = jnp.where(usable, s * SCALE, -jnp.inf)
        sbuf[c] = s
        mbuf[...] = jnp.maximum(mbuf[...], s)
        return carry

    lax.fori_loop(0, chunks, score, 0)
    highest = jnp.maximum(
        jnp.max(mbuf[...], axis=1, keepdims=True), jnp.max(fresh_scores, axis=1, keepdims=True)
    )
    new_w = jnp.exp(fresh_scores - highest)
    new_sum = jnp.sum(new_w, axis=1, keepdims=True)
    acc[...] = jnp.dot(new_w.astype(jnp.bfloat16), new_lat, preferred_element_type=jnp.float32)
    mbuf[...] = jnp.zeros_like(mbuf)

    def weigh(c, carry):
        w = jnp.exp(sbuf[c] - highest)
        mbuf[...] += w
        acc[...] += jnp.dot(w.astype(jnp.bfloat16), kbuf[c], preferred_element_type=jnp.float32)
        return carry

    lax.fori_loop(0, chunks, weigh, 0)
    total = new_sum + jnp.sum(mbuf[...], axis=1, keepdims=True)
    obuf[...] = (acc[...] / total).astype(jnp.bfloat16)
    outs = [out_copy(t, obuf.at[pl.ds(t * heads, heads)], qsem.at[t]) for t in range(steps)]
    for copy in outs:
        copy.start()
    for copy in outs:
        copy.wait()


def plain_copies(lat, rope, pick, block):
    def copies(source, j, kbuf, rbuf, ksem, rsem):
        b = pick(source)
        c, side = j // 2, pl.multiple_of((j % 2) * block, block)
        return [
            pltpu.make_async_copy(lat.at[b], kbuf.at[c, pl.ds(side, block)], ksem.at[j]),
            pltpu.make_async_copy(rope.at[b], rbuf.at[c, :, pl.ds(side, block)], rsem.at[j, 0]),
        ]

    return copies


def every(copies):
    def each(j, source, what, *bufs):
        for copy in copies(source, j, *bufs):
            what(copy)

    return each


def packed_copies(got, pick, block, rope_rows, latent):
    parts = latent // block

    def copies(source, j, kbuf, rbuf, ksem, rsem):
        e = pick(source)
        c, side = j // 2, pl.multiple_of((j % 2) * block, block)
        out = [
            pltpu.make_async_copy(
                got.at[e, pl.ds(0, block)], kbuf.at[c, pl.ds(side, block)], ksem.at[j]
            )
        ]
        for g in range(parts):
            out.append(
                pltpu.make_async_copy(
                    got.at[e, pl.ds(block, rope_rows), pl.ds(g * block, block)],
                    rbuf.at[c, pl.ds(g * rope_rows, rope_rows), pl.ds(side, block)],
                    rsem.at[j, g],
                )
            )
        return out

    return copies


def chunk_spans(blocks):
    sizes = []
    while blocks > 0:
        sizes.append(min(3 if not sizes or blocks == 3 else 2, blocks))
        blocks -= sizes[-1]
    return sizes


def cost(plan):
    keys = plan.most * plan.block
    return pl.CostEstimate(
        flops=2 * plan.rows * keys * (2 * plan.latent + plan.rope) // 2,
        bytes_accessed=2 * keys * (plan.latent + plan.rope) // 2,
        transcendentals=plan.rows * keys // 2,
    )


def resident_kernel(plan, slot, table, length, q_lat, q_rope, fresh, lat, rope, out, *scr):
    used = length[0]
    attention(
        plan, scr, q_lat.at[slot], q_rope.at[slot], fresh.at[slot],
        every(plain_copies(lat, rope, lambda j: table[0, j], plan.block)),
        ceil_div(used, plan.block), used, False,
        lambda t, src, sem: pltpu.make_async_copy(src, out.at[t], sem),
    )


def migrated_kernel(plan, slot, sizes, length, q_lat, q_rope, fresh, *refs):
    chunks, out, scr = refs[: len(sizes)], refs[len(sizes) + 1], refs[len(sizes) + 2 :]
    used = length[0]
    rope_rows = plan.rope * plan.block // plan.latent
    starts = [sum(sizes[:i]) for i in range(len(sizes))]

    def each(j, source, what, kbuf, rbuf, ksem, rsem):
        for ref, first, size in zip(chunks, starts, sizes, strict=True):

            @pl.when((source >= first) & (source < first + size))
            def _(ref=ref, first=first):
                for copy in packed_copies(ref, lambda e: e - first, plan.block, rope_rows, plan.latent)(
                    source, j, kbuf, rbuf, ksem, rsem
                ):
                    what(copy)

    attention(
        plan, scr, q_lat.at[slot], q_rope.at[slot], fresh.at[slot], each,
        ceil_div(used, plan.block), used, False,
        lambda t, src, sem: pltpu.make_async_copy(src, out.at[slot, t], sem),
    )


def arriving_kernel(plan, slot, index, arrived, q_lat, q_rope, fresh, got, ready, out, rbuf, rsem, *scr):
    fetch = pltpu.make_async_copy(ready, rbuf, rsem.at[0])
    fetch.start()
    used = arrived[0]
    fetch.wait()
    put = pltpu.make_async_copy(rbuf, out.at[slot - 1], rsem.at[1])
    put.start()
    attention(
        plan, scr, q_lat.at[slot], q_rope.at[slot], fresh.at[slot],
        every(packed_copies(got, lambda j: index[j], plan.block, plan.rope * plan.block // plan.latent, plan.latent)),
        used, used * plan.block, True,
        lambda t, src, sem: pltpu.make_async_copy(src, out.at[slot, t], sem),
    )
    put.wait()


def pack_kernel(table, fill, lat, rope, out, lbuf, rbuf, pbuf, lsem, rsem, osem):
    blocks, block, latent = lat.shape
    rows = pbuf.shape[1]
    small = pltpu.make_async_copy(rope, rbuf, rsem)
    pulls = [pltpu.make_async_copy(lat.at[b], lbuf.at[b], lsem.at[b]) for b in range(blocks)]
    small.start()
    for pull in pulls:
        pull.start()
    small.wait()
    first = lax.broadcasted_iota(jnp.int32, rope.shape[1:], 0) == 0
    token = lax.broadcasted_iota(jnp.int32, rope.shape[1:], 1)
    for b in range(blocks):
        marked = jnp.where(first & (token >= fill[b]), MARK, rbuf[b].astype(jnp.float32)).astype(jnp.bfloat16)
        for g in range(latent // block):
            pbuf[b, :, g * block : (g + 1) * block] = marked[g * rows : (g + 1) * rows]
    for pull in pulls:
        pull.wait()

    def each(o, what):
        b = table[o]

        @pl.when(b >= 0)
        def _():
            for copy in (
                pltpu.make_async_copy(lbuf.at[b], out.at[o, pl.ds(0, block)], osem.at[b, 0]),
                pltpu.make_async_copy(pbuf.at[b], out.at[o, pl.ds(block, rows)], osem.at[b, 1]),
            ):
                what(copy)

    def launch(o, carry):
        each(o, lambda copy: copy.start())
        return carry

    def settle(o, carry):
        each(o, lambda copy: copy.wait())
        return carry

    lax.fori_loop(0, out.shape[0], launch, 0)
    lax.fori_loop(0, out.shape[0], settle, 0)


def chunk_kernel(sizes, lat, rope, *refs):
    outs = refs[: len(sizes)]
    lbuf, rbuf, pbuf, lsem, rsem, osem = refs[len(sizes) :]
    blocks, block, latent = lat.shape
    rows = pbuf.shape[1]
    small = pltpu.make_async_copy(rope, rbuf, rsem)
    small.start()
    starts = [sum(sizes[:i]) for i in range(len(sizes))]
    spans = [pl.ds(first, size) for first, size in zip(starts, sizes, strict=True)]
    pulls = [pltpu.make_async_copy(lat.at[span], lbuf.at[span], lsem.at[i]) for i, span in enumerate(spans)]
    for pull in pulls:
        pull.start()
    small.wait()
    for b in range(blocks):
        for g in range(latent // block):
            pbuf[b, :, g * block : (g + 1) * block] = rbuf[b, g * rows : (g + 1) * rows]
    puts = []
    for i, (span, out) in enumerate(zip(spans, outs, strict=True)):
        pulls[i].wait()
        puts.append(pltpu.make_async_copy(lbuf.at[span], out.at[:, pl.ds(0, block)], osem.at[i, 0]))
        puts.append(pltpu.make_async_copy(pbuf.at[span], out.at[:, pl.ds(block, rows)], osem.at[i, 1]))
        for put in puts[-2:]:
            put.start()
    for put in puts:
        put.wait()


def shards(
    res_lat, res_rope, res_table, res_len, out_lat, out_rope, out_fill, send_table, arr_index,
    arr_count, mig_lat, mig_rope, mig_len, mig_bit, q_lat, q_rope, new_kv,
):
    count = lax.axis_size("dp")
    bits = count.bit_length() - 1
    slots, steps, heads, latent = q_lat.shape
    rope = q_rope.shape[2]
    block = res_lat.shape[1]
    requests = res_len.shape[0]
    assert requests == 1 and send_table.shape[0] == count
    make = functools.partial(Plan, steps=steps, heads=heads, latent=latent, rope=rope, block=block)
    rows = rope * block // latent
    blocks = out_lat.shape[0]

    packed = pl.pallas_call(
        pack_kernel,
        out_shape=jax.ShapeDtypeStruct((count, block + rows, latent), jnp.bfloat16),
        in_specs=[SMEM, SMEM, ANY, ANY],
        out_specs=ANY,
        scratch_shapes=[
            pltpu.VMEM((blocks, block, latent), jnp.bfloat16),
            pltpu.VMEM((blocks, rope, block), jnp.bfloat16),
            pltpu.VMEM((blocks, rows, latent), jnp.bfloat16),
            DMA((blocks,)), DMA, DMA((blocks, 2)),
        ],
        name="pack",
    )(send_table, out_fill, out_lat, out_rope)
    got = lax.all_to_all(packed, "dp", split_axis=0, concat_axis=0, tiled=True)

    held = mig_lat.shape[0]
    sizes = chunk_spans(held)
    mig_lat, mig_rope, packed = lax.optimization_barrier((mig_lat, mig_rope, packed))
    chunks = pl.pallas_call(
        functools.partial(chunk_kernel, sizes),
        out_shape=[jax.ShapeDtypeStruct((n, block + rows, latent), jnp.bfloat16) for n in sizes],
        in_specs=[ANY, ANY],
        out_specs=[ANY] * len(sizes),
        scratch_shapes=[
            pltpu.VMEM((held, block, latent), jnp.bfloat16),
            pltpu.VMEM((held, rope, block), jnp.bfloat16),
            pltpu.VMEM((held, rows, latent), jnp.bfloat16),
            DMA((len(sizes),)), DMA, DMA((len(sizes), 2)),
        ],
        name="chunk",
    )(mig_lat, mig_rope)
    chunks = list(chunks)

    ends = [sum(sizes[: i + 1]) * block for i in range(len(sizes))]

    def level_of(one, other):
        longest = jnp.maximum(one, other)[0]
        return sum((longest > end).astype(jnp.int32) for end in ends[:-1])

    def swapper(bit):
        route = [(i, i ^ 1 << bit) for i in range(count)]
        return lambda x: lax.ppermute(x, "dp", route)

    def near(bit):
        swap = swapper(bit)

        def branch(length, chunks):
            other = swap(length)

            def sending(k):
                return lambda chunks: [swap(x) if i <= k else x for i, x in enumerate(chunks)]

            level = level_of(length, other)
            return other, lax.switch(level, [sending(k) for k in range(len(sizes))], chunks)

        return branch

    far = bits - 1
    length, chunks = lax.switch(
        mig_bit[0] + 1,
        [lambda length, chunks: (length, chunks)]
        + [near(bit) for bit in range(far)]
        + [lambda length, chunks: (swapper(far)(length), chunks)],
        mig_len, chunks,
    )

    plan = make(res_table.shape[1])
    ready = pl.pallas_call(
        functools.partial(resident_kernel, plan, 0),
        out_shape=jax.ShapeDtypeStruct((steps, heads, latent), jnp.bfloat16),
        in_specs=[SMEM, SMEM, ANY, ANY, ANY, ANY, ANY],
        out_specs=ANY,
        scratch_shapes=plan.scratch(),
        cost_estimate=cost(plan),
        name="resident",
    )(res_table, res_len, q_lat, q_rope, new_kv, res_lat, res_rope)

    def finish(k):
        def branch(index, arrived, length, q_lat, q_rope, new_kv, got, ready, chunks):
            shape = jax.ShapeDtypeStruct((slots, steps, heads, latent), jnp.bfloat16)
            chunks = [swapper(far)(x) if i < k else x for i, x in enumerate(chunks)]
            plan = make(index.shape[0])
            base = pl.pallas_call(
                functools.partial(arriving_kernel, plan, requests),
                out_shape=shape,
                in_specs=[SMEM, SMEM, ANY, ANY, ANY, ANY, ANY],
                out_specs=ANY,
                scratch_shapes=[pltpu.VMEM((steps, heads, latent), jnp.bfloat16), DMA((2,))] + plan.scratch(),
                cost_estimate=cost(plan),
                name="arriving",
            )(index, arrived, q_lat, q_rope, new_kv, got, ready)
            plan = make(held)
            return pl.pallas_call(
                functools.partial(migrated_kernel, plan, requests + 1, sizes),
                out_shape=shape,
                in_specs=[SMEM] + [ANY] * (4 + len(sizes)),
                out_specs=ANY,
                scratch_shapes=plan.scratch(),
                input_output_aliases={4 + len(sizes): 0},
                cost_estimate=cost(plan),
                name="migrated",
            )(length, q_lat, q_rope, new_kv, *chunks, base)

        return branch

    last = jnp.where(mig_bit[0] == far, 1 + level_of(mig_len, length), 0)
    return lax.switch(
        last,
        [finish(k) for k in range(len(sizes) + 1)],
        arr_index, arr_count, length, q_lat, q_rope, new_kv, got, ready, chunks,
    )


def solution(mesh):
    whole = P(("groups", "dp"))
    return jax.shard_map(shards, mesh=mesh, in_specs=(whole,) * 17, out_specs=whole, check_vma=False)
```

```python
import functools

import jax
import jax.numpy as jnp
from jax import lax
from jax.experimental import pallas as pl
from jax.experimental.pallas import tpu as pltpu
from jax.sharding import PartitionSpec as P

SCALE = 192.0 ** (-0.5)
MARK = 1e30
LIMIT = 1e20
ANY = pl.BlockSpec(memory_space=pl.ANY)
SMEM = pl.BlockSpec(memory_space=pltpu.SMEM)
DMA = pltpu.SemaphoreType.DMA


def contract_last(a, b):
    return lax.dot_general(a, b, (((1,), (1,)), ((), ())), preferred_element_type=jnp.float32)


def ceil_div(a, b):
    return (a + b - 1) // b


class Plan:
    def __init__(self, most, steps, heads, latent, rope, block, visitor=False):
        self.visitor = visitor
        self.most = most + most % 2
        self.steps, self.heads, self.latent, self.rope, self.block = steps, heads, latent, rope, block
        self.rows = steps * heads
        self.pair = 2 * block

    def scratch(self):
        chunks = self.most // 2
        return [
            pltpu.VMEM((self.rows, self.latent), jnp.bfloat16),
            pltpu.VMEM((self.steps, self.rope, self.heads), jnp.bfloat16),
            pltpu.VMEM((self.rows, self.rope), jnp.bfloat16),
            pltpu.VMEM((16, self.latent) if self.visitor else (self.steps, self.latent + self.rope), jnp.bfloat16),
            pltpu.VMEM((self.block, self.latent + self.rope), jnp.float32),
            pltpu.VMEM((chunks, self.pair, self.latent), jnp.bfloat16),
            pltpu.VMEM((chunks, self.rope, self.pair), jnp.bfloat16),
            pltpu.VMEM((chunks, self.rows, self.pair), jnp.float32),
            pltpu.VMEM((self.rows, self.pair), jnp.float32),
            pltpu.VMEM((self.rows, self.latent), jnp.float32),
            pltpu.VMEM((self.rows, self.latent), jnp.bfloat16),
            DMA((self.steps + 3,)),
            DMA((self.most,)),
            DMA((self.most, 4)),
        ]


def own_queries(q_lat, q_rope, fresh):
    def copies(plan, qbuf, qrbuf, newraw, sem):
        steps, heads = plan.steps, plan.heads
        out = [
            pltpu.make_async_copy(q_lat.at[t], qbuf.at[pl.ds(t * heads, heads)], sem.at[t])
            for t in range(steps)
        ]
        out.append(pltpu.make_async_copy(q_rope, qrbuf, sem.at[steps]))
        out.append(pltpu.make_async_copy(fresh, newraw, sem.at[steps + 1]))
        return out

    return copies


def visiting_queries(payload):
    def copies(plan, qbuf, qrbuf, newraw, sem):
        rows, heads = plan.rows, plan.heads
        out = [
            pltpu.make_async_copy(
                payload.at[pl.ds(rows, plan.rope), pl.ds(t * heads, heads)], qrbuf.at[t], sem.at[t]
            )
            for t in range(plan.steps)
        ]
        out.append(pltpu.make_async_copy(payload.at[pl.ds(0, rows)], qbuf, sem.at[plan.steps]))
        out.append(
            pltpu.make_async_copy(payload.at[pl.ds(rows + plan.rope, 16)], newraw, sem.at[plan.steps + 1])
        )
        return out

    return copies


def attention(plan, scr, queries, block_copies, count, limit, marked, out_copy):
    (qbuf, qrbuf, qrt, newraw, newpad, kbuf, rbuf, sbuf, mbuf, acc, obuf, qsem, ksem, rsem) = scr
    steps, heads, latent, pair = plan.steps, plan.heads, plan.latent, plan.pair
    copies = queries(plan, qbuf, qrbuf, newraw, qsem)
    for copy in copies:
        copy.start()
    chunks = ceil_div(count, 2)

    def each(j, what):
        block_copies(j, jnp.minimum(j, count - 1), what, kbuf, rbuf, ksem, rsem)

    def launch(j, carry):
        each(j, lambda copy: copy.start())
        return carry

    lax.fori_loop(0, 2 * chunks, launch, 0)
    for copy in copies:
        copy.wait()
    for t in range(steps):
        qrt[pl.ds(t * heads, heads), :] = qrbuf[t].astype(jnp.float32).T.astype(jnp.bfloat16)
    newpad[...] = jnp.zeros_like(newpad)
    if plan.visitor:
        newpad[0:steps, :latent] = newraw[...].astype(jnp.float32)[0:steps]
        newpad[0:steps, latent:] = newraw[...].astype(jnp.float32)[8 : 8 + steps, : plan.rope]
    else:
        newpad[0:steps, :] = newraw[...].astype(jnp.float32)
    new_lat = newpad[:, :latent].astype(jnp.bfloat16)
    new_rope = newpad[:, latent:].astype(jnp.bfloat16)
    fresh_scores = (contract_last(qbuf[...], new_lat) + contract_last(qrt[...], new_rope)) * SCALE
    step_of = lax.broadcasted_iota(jnp.int32, (plan.rows, plan.block), 0) // heads
    new_of = lax.broadcasted_iota(jnp.int32, (plan.rows, plan.block), 1)
    fresh_scores = jnp.where(new_of <= step_of, fresh_scores, -jnp.inf)
    mbuf[...] = jnp.full_like(mbuf, -jnp.inf)

    def score(c, carry):
        each(2 * c, lambda copy: copy.wait())
        each(2 * c + 1, lambda copy: copy.wait())
        rope = rbuf[c]
        s = contract_last(qbuf[...], kbuf[c]) + jnp.dot(
            qrt[...], rope, preferred_element_type=jnp.float32
        )
        usable = lax.broadcasted_iota(jnp.int32, (1, pair), 1) + c * pair < limit
        if marked:
            usable = usable & (rope[0:1, :].astype(jnp.float32) < LIMIT)
        s = jnp.where(usable, s * SCALE, -jnp.inf)
        sbuf[c] = s
        mbuf[...] = jnp.maximum(mbuf[...], s)
        return carry

    lax.fori_loop(0, chunks, score, 0)
    highest = jnp.maximum(
        jnp.max(mbuf[...], axis=1, keepdims=True), jnp.max(fresh_scores, axis=1, keepdims=True)
    )
    new_w = jnp.exp(fresh_scores - highest)
    new_sum = jnp.sum(new_w, axis=1, keepdims=True)
    acc[...] = jnp.dot(new_w.astype(jnp.bfloat16), new_lat, preferred_element_type=jnp.float32)
    mbuf[...] = jnp.zeros_like(mbuf)

    def weigh(c, carry):
        w = jnp.exp(sbuf[c] - highest)
        mbuf[...] += w
        acc[...] += jnp.dot(w.astype(jnp.bfloat16), kbuf[c], preferred_element_type=jnp.float32)
        return carry

    lax.fori_loop(0, chunks, weigh, 0)
    total = new_sum + jnp.sum(mbuf[...], axis=1, keepdims=True)
    obuf[...] = (acc[...] / total).astype(jnp.bfloat16)
    outs = [out_copy(t, obuf.at[pl.ds(t * heads, heads)], qsem.at[t]) for t in range(steps)]
    for copy in outs:
        copy.start()
    for copy in outs:
        copy.wait()


def plain_copies(lat, rope, pick, block):
    def copies(source, j, kbuf, rbuf, ksem, rsem):
        b = pick(source)
        c, side = j // 2, pl.multiple_of((j % 2) * block, block)
        return [
            pltpu.make_async_copy(lat.at[b], kbuf.at[c, pl.ds(side, block)], ksem.at[j]),
            pltpu.make_async_copy(rope.at[b], rbuf.at[c, :, pl.ds(side, block)], rsem.at[j, 0]),
        ]

    return copies


def every(copies):
    def each(j, source, what, *bufs):
        for copy in copies(source, j, *bufs):
            what(copy)

    return each


def packed_copies(got, pick, block, rope_rows, latent):
    parts = latent // block

    def copies(source, j, kbuf, rbuf, ksem, rsem):
        e = pick(source)
        c, side = j // 2, pl.multiple_of((j % 2) * block, block)
        out = [
            pltpu.make_async_copy(
                got.at[e, pl.ds(0, block)], kbuf.at[c, pl.ds(side, block)], ksem.at[j]
            )
        ]
        for g in range(parts):
            out.append(
                pltpu.make_async_copy(
                    got.at[e, pl.ds(block, rope_rows), pl.ds(g * block, block)],
                    rbuf.at[c, pl.ds(g * rope_rows, rope_rows), pl.ds(side, block)],
                    rsem.at[j, g],
                )
            )
        return out

    return copies


def chunk_spans(blocks):
    sizes = []
    while blocks > 0:
        sizes.append(min(3 if not sizes or blocks == 3 else 2, blocks))
        blocks -= sizes[-1]
    return sizes


def cost(plan):
    keys = plan.most * plan.block
    return pl.CostEstimate(
        flops=2 * plan.rows * keys * (2 * plan.latent + plan.rope) // 2,
        bytes_accessed=2 * keys * (plan.latent + plan.rope) // 2,
        transcendentals=plan.rows * keys // 2,
    )


def resident_kernel(plan, slot, table, length, q_lat, q_rope, fresh, lat, rope, out, *scr):
    used = length[0]
    attention(
        plan, scr, own_queries(q_lat.at[slot], q_rope.at[slot], fresh.at[slot]),
        every(plain_copies(lat, rope, lambda j: table[0, j], plan.block)),
        ceil_div(used, plan.block), used, False,
        lambda t, src, sem: pltpu.make_async_copy(src, out.at[t], sem),
    )


def chunked(plan, sizes, chunks):
    rope_rows = plan.rope * plan.block // plan.latent
    starts = [sum(sizes[:i]) for i in range(len(sizes))]

    def each(j, source, what, *bufs):
        for ref, first, size in zip(chunks, starts, sizes, strict=True):

            @pl.when((source >= first) & (source < first + size))
            def _(ref=ref, first=first):
                for copy in packed_copies(ref, lambda e: e - first, plan.block, rope_rows, plan.latent)(source, j, *bufs):
                    what(copy)

    if len(sizes) == 1:
        return every(packed_copies(chunks[0], lambda e: e, plan.block, rope_rows, plan.latent))
    return each


def migrated_kernel(plan, slot, sizes, length, q_lat, q_rope, fresh, *refs):
    chunks, out, scr = refs[: len(sizes)], refs[len(sizes) + 1], refs[len(sizes) + 2 :]
    used = length[0]
    attention(
        plan, scr, own_queries(q_lat.at[slot], q_rope.at[slot], fresh.at[slot]), chunked(plan, sizes, chunks),
        ceil_div(used, plan.block), used, False,
        lambda t, src, sem: pltpu.make_async_copy(src, out.at[slot, t], sem),
    )


def visited_kernel(plan, sizes, length, payload, *refs):
    chunks, out, scr = refs[: len(sizes)], refs[len(sizes)], refs[len(sizes) + 1 :]
    used = length[0]
    attention(
        plan, scr, visiting_queries(payload), chunked(plan, sizes, chunks),
        ceil_div(used, plan.block), used, False,
        lambda t, src, sem: pltpu.make_async_copy(src, out.at[t], sem),
    )


def place_kernel(slot, back, base, out, buf, sem):
    del base
    for copy in (pltpu.make_async_copy(back, buf, sem.at[0]), pltpu.make_async_copy(buf, out.at[slot], sem.at[1])):
        copy.start()
        copy.wait()


def arriving_kernel(plan, slot, index, arrived, q_lat, q_rope, fresh, got, ready, out, rbuf, rsem, *scr):
    fetch = pltpu.make_async_copy(ready, rbuf, rsem.at[0])
    fetch.start()
    used = arrived[0]
    fetch.wait()
    put = pltpu.make_async_copy(rbuf, out.at[slot - 1], rsem.at[1])
    put.start()
    attention(
        plan, scr, own_queries(q_lat.at[slot], q_rope.at[slot], fresh.at[slot]),
        every(packed_copies(got, lambda j: index[j], plan.block, plan.rope * plan.block // plan.latent, plan.latent)),
        used, used * plan.block, True,
        lambda t, src, sem: pltpu.make_async_copy(src, out.at[slot, t], sem),
    )
    put.wait()


def pack_kernel(table, fill, lat, rope, out, lbuf, rbuf, pbuf, lsem, rsem, osem):
    blocks, block, latent = lat.shape
    rows = pbuf.shape[1]
    small = pltpu.make_async_copy(rope, rbuf, rsem)
    pulls = [pltpu.make_async_copy(lat.at[b], lbuf.at[b], lsem.at[b]) for b in range(blocks)]
    small.start()
    for pull in pulls:
        pull.start()
    small.wait()
    first = lax.broadcasted_iota(jnp.int32, rope.shape[1:], 0) == 0
    token = lax.broadcasted_iota(jnp.int32, rope.shape[1:], 1)
    for b in range(blocks):
        marked = jnp.where(first & (token >= fill[b]), MARK, rbuf[b].astype(jnp.float32)).astype(jnp.bfloat16)
        for g in range(latent // block):
            pbuf[b, :, g * block : (g + 1) * block] = marked[g * rows : (g + 1) * rows]
    for pull in pulls:
        pull.wait()

    def each(o, what):
        b = table[o]

        @pl.when(b >= 0)
        def _():
            for copy in (
                pltpu.make_async_copy(lbuf.at[b], out.at[o, pl.ds(0, block)], osem.at[b, 0]),
                pltpu.make_async_copy(pbuf.at[b], out.at[o, pl.ds(block, rows)], osem.at[b, 1]),
            ):
                what(copy)

    def launch(o, carry):
        each(o, lambda copy: copy.start())
        return carry

    def settle(o, carry):
        each(o, lambda copy: copy.wait())
        return carry

    lax.fori_loop(0, out.shape[0], launch, 0)
    lax.fori_loop(0, out.shape[0], settle, 0)


def chunk_kernel(spans, slot, lat, rope, q_lat, q_rope, fresh, *refs):
    outs, payload = refs[: len(spans)], refs[len(spans)]
    lbuf, rbuf, pbuf, qbuf, qrbuf, fbuf, mbuf, sem, osem, qsem = refs[len(spans) + 1 :]
    blocks, block, latent = lat.shape
    steps, heads = qbuf.shape[0] // block, block
    rows = pbuf.shape[1]
    wide = steps * heads
    pulls = [
        pltpu.make_async_copy(rope, rbuf, sem.at[0]),
        pltpu.make_async_copy(q_rope.at[slot], qrbuf, sem.at[1]),
        pltpu.make_async_copy(fresh.at[slot], fbuf, sem.at[2]),
        pltpu.make_async_copy(lat, lbuf, sem.at[3]),
    ]
    pulls += [
        pltpu.make_async_copy(q_lat.at[slot, t], qbuf.at[pl.ds(t * heads, heads)], sem.at[4 + t])
        for t in range(steps)
    ]
    for pull in pulls:
        pull.start()
    for pull in pulls:
        pull.wait()
    for b in range(blocks):
        for g in range(latent // block):
            pbuf[b, :, g * block : (g + 1) * block] = rbuf[b, g * rows : (g + 1) * rows]
    puts = []
    for i, ((first, size), out) in enumerate(zip(spans, outs, strict=True)):
        span = pl.ds(first, size)
        puts.append(pltpu.make_async_copy(lbuf.at[span], out.at[:, pl.ds(0, block)], osem.at[i, 0]))
        puts.append(pltpu.make_async_copy(pbuf.at[span], out.at[:, pl.ds(block, rows)], osem.at[i, 1]))
    mbuf[...] = jnp.zeros_like(mbuf)
    new = fbuf[...].astype(jnp.float32)
    mbuf[0:steps, :] = new[:, :latent]
    mbuf[8 : 8 + steps, : new.shape[1] - latent] = new[:, latent:]
    tail = qrbuf.shape[1]
    qbuf[wide + tail : wide + tail + 16, :] = mbuf[...].astype(jnp.bfloat16)
    for t in range(steps):
        qbuf[wide : wide + tail, t * heads : (t + 1) * heads] = qrbuf[t]
    puts.append(pltpu.make_async_copy(qbuf, payload, qsem))
    for put in puts:
        put.start()
    for put in puts:
        put.wait()


def shards(
    res_lat, res_rope, res_table, res_len, out_lat, out_rope, out_fill, send_table, arr_index,
    arr_count, mig_lat, mig_rope, mig_len, mig_bit, q_lat, q_rope, new_kv,
):
    count = lax.axis_size("dp")
    bits = count.bit_length() - 1
    slots, steps, heads, latent = q_lat.shape
    rope = q_rope.shape[2]
    block = res_lat.shape[1]
    requests = res_len.shape[0]
    assert requests == 1 and send_table.shape[0] == count
    make = functools.partial(Plan, steps=steps, heads=heads, latent=latent, rope=rope, block=block)
    rows = rope * block // latent
    blocks = out_lat.shape[0]

    packed = pl.pallas_call(
        pack_kernel,
        out_shape=jax.ShapeDtypeStruct((count, block + rows, latent), jnp.bfloat16),
        in_specs=[SMEM, SMEM, ANY, ANY],
        out_specs=ANY,
        scratch_shapes=[
            pltpu.VMEM((blocks, block, latent), jnp.bfloat16),
            pltpu.VMEM((blocks, rope, block), jnp.bfloat16),
            pltpu.VMEM((blocks, rows, latent), jnp.bfloat16),
            DMA((blocks,)), DMA, DMA((blocks, 2)),
        ],
        name="pack",
    )(send_table, out_fill, out_lat, out_rope)
    got = lax.all_to_all(packed, "dp", split_axis=0, concat_axis=0, tiled=True)

    plan = make(res_table.shape[1])
    res_table, packed = lax.optimization_barrier((res_table, packed))
    ready = pl.pallas_call(
        functools.partial(resident_kernel, plan, 0),
        out_shape=jax.ShapeDtypeStruct((steps, heads, latent), jnp.bfloat16),
        in_specs=[SMEM, SMEM, ANY, ANY, ANY, ANY, ANY],
        out_specs=ANY,
        scratch_shapes=plan.scratch(),
        cost_estimate=cost(plan),
        name="resident",
    )(res_table, res_len, q_lat, q_rope, new_kv, res_lat, res_rope)

    held = mig_lat.shape[0]
    sizes = chunk_spans(held)
    levels = [n for n in (2, 4, 6, 8) if n < held]
    mig_lat, mig_rope, packed = lax.optimization_barrier((mig_lat, mig_rope, packed))
    spans = [(sum(sizes[:i]), n) for i, n in enumerate(sizes)] + [(0, n) for n in levels]
    mail = steps * heads + rope + 16
    *pieces, payload = pl.pallas_call(
        functools.partial(chunk_kernel, spans, requests + 1),
        out_shape=[jax.ShapeDtypeStruct((n, block + rows, latent), jnp.bfloat16) for _, n in spans]
        + [jax.ShapeDtypeStruct((mail, latent), jnp.bfloat16)],
        in_specs=[ANY] * 5,
        out_specs=[ANY] * (len(spans) + 1),
        scratch_shapes=[
            pltpu.VMEM((held, block, latent), jnp.bfloat16),
            pltpu.VMEM((held, rope, block), jnp.bfloat16),
            pltpu.VMEM((held, rows, latent), jnp.bfloat16),
            pltpu.VMEM((mail, latent), jnp.bfloat16),
            pltpu.VMEM((steps, rope, heads), jnp.bfloat16),
            pltpu.VMEM(new_kv.shape[1:], jnp.bfloat16),
            pltpu.VMEM((16, latent), jnp.float32),
            DMA((4 + steps,)), DMA((len(spans), 2)), DMA,
        ],
        name="chunk",
    )(mig_lat, mig_rope, q_lat, q_rope, new_kv)
    chunks, prefixes = pieces[: len(sizes)], pieces[len(sizes) :]
    ready, chunks = lax.optimization_barrier((ready, chunks))

    ends = [sum(sizes[: i + 1]) * block for i in range(len(sizes))]

    def level_of(one, other):
        longest = jnp.maximum(one, other)[0]
        return sum((longest > end).astype(jnp.int32) for end in ends[:-1])

    def swapper(bit):
        route = [(i, i ^ 1 << bit) for i in range(count)]
        return lambda x: lax.ppermute(x, "dp", route)

    def near(bit):
        swap = swapper(bit)

        def branch(length, chunks):
            other = swap(length)

            def sending(k):
                return lambda chunks: [swap(x) if i <= k else x for i, x in enumerate(chunks)]

            level = level_of(length, other)
            return other, lax.switch(level, [sending(k) for k in range(len(sizes))], chunks)

        return branch

    far = bits - 1
    length, chunks = lax.switch(
        mig_bit[0] + 1,
        [lambda length, chunks: (length, chunks)]
        + [near(bit) for bit in range(far)]
        + [lambda length, chunks: (swapper(far)(length), chunks)],
        mig_len, chunks,
    )

    whole = jax.ShapeDtypeStruct((slots, steps, heads, latent), jnp.bfloat16)

    def arrive(index, arrived, got, ready, q_lat, q_rope, new_kv):
        plan = make(index.shape[0])
        return pl.pallas_call(
            functools.partial(arriving_kernel, plan, requests),
            out_shape=whole,
            in_specs=[SMEM, SMEM, ANY, ANY, ANY, ANY, ANY],
            out_specs=ANY,
            scratch_shapes=[pltpu.VMEM((steps, heads, latent), jnp.bfloat16), DMA((2,))] + plan.scratch(),
            cost_estimate=cost(plan),
            name="arriving",
        )(index, arrived, q_lat, q_rope, new_kv, got, ready)

    def migrate(length, q_lat, q_rope, new_kv, sizes, chunks, base):
        plan = make(sum(sizes))
        return pl.pallas_call(
            functools.partial(migrated_kernel, plan, requests + 1, sizes),
            out_shape=whole,
            in_specs=[SMEM] + [ANY] * (4 + len(sizes)),
            out_specs=ANY,
            scratch_shapes=plan.scratch(),
            input_output_aliases={4 + len(sizes): 0},
            cost_estimate=cost(plan),
            name="migrated",
        )(length, q_lat, q_rope, new_kv, *chunks, base)

    swap = swapper(far)

    def local(arrival, queries, own, length, chunks, prefixes, payload):
        base = arrive(*arrival, *queries)
        return migrate(length, *queries, sizes, chunks, base)

    def shipped(k):
        def branch(arrival, queries, own, length, chunks, prefixes, payload):
            cache = swap(prefixes[k])
            base = arrive(*arrival, *queries)
            return migrate(length, *queries, [levels[k]], [cache], base)

        return branch

    def visited(arrival, queries, own, length, chunks, prefixes, payload):
        plan = make(held, visitor=True)
        result = pl.pallas_call(
            functools.partial(visited_kernel, plan, sizes),
            out_shape=jax.ShapeDtypeStruct((steps, heads, latent), jnp.bfloat16),
            in_specs=[SMEM] + [ANY] * (1 + len(sizes)),
            out_specs=ANY,
            scratch_shapes=plan.scratch(),
            cost_estimate=cost(plan),
            name="visited",
        )(own, swap(payload), *chunks)
        back = swap(result)
        base = arrive(*arrival, *queries)
        return pl.pallas_call(
            functools.partial(place_kernel, requests + 1),
            out_shape=whole,
            in_specs=[ANY, ANY],
            out_specs=ANY,
            scratch_shapes=[pltpu.VMEM((steps, heads, latent), jnp.bfloat16), DMA((2,))],
            input_output_aliases={1: 0},
            name="place",
        )(back, base)

    longest = jnp.maximum(mig_len, length)[0]
    step = 1 + sum((longest > n * block).astype(jnp.int32) for n in levels)
    return lax.switch(
        jnp.where(mig_bit[0] == far, step, 0),
        [local] + [shipped(k) for k in range(len(levels))] + [visited],
        (arr_index, arr_count, got, ready), (q_lat, q_rope, new_kv), mig_len, length, chunks, prefixes, payload,
    )


def solution(mesh):
    whole = P(("groups", "dp"))
    return jax.shard_map(shards, mesh=mesh, in_specs=(whole,) * 17, out_specs=whole, check_vma=False)
```

```python
import functools

import jax
import jax.numpy as jnp
from jax import lax
from jax.experimental import pallas as pl
from jax.experimental.pallas import tpu as pltpu
from jax.sharding import PartitionSpec as P

SCALE = 192.0 ** (-0.5)
MARK = 1e30
LIMIT = 1e20
ANY = pl.BlockSpec(memory_space=pl.ANY)
SMEM = pl.BlockSpec(memory_space=pltpu.SMEM)
DMA = pltpu.SemaphoreType.DMA


def contract_last(a, b):
    return lax.dot_general(a, b, (((1,), (1,)), ((), ())), preferred_element_type=jnp.float32)


def ceil_div(a, b):
    return (a + b - 1) // b


class Plan:
    def __init__(self, most, steps, heads, latent, rope, block, visitor=False):
        self.visitor = visitor
        self.most = most + most % 2
        self.steps, self.heads, self.latent, self.rope, self.block = steps, heads, latent, rope, block
        self.rows = steps * heads
        self.pair = 2 * block

    def scratch(self):
        chunks = self.most // 2
        return [
            pltpu.VMEM((self.rows, self.latent), jnp.bfloat16),
            pltpu.VMEM((self.steps, self.rope, self.heads), jnp.bfloat16),
            pltpu.VMEM((self.rows, self.rope), jnp.bfloat16),
            pltpu.VMEM((16, self.latent) if self.visitor else (self.steps, self.latent + self.rope), jnp.bfloat16),
            pltpu.VMEM((self.block, self.latent + self.rope), jnp.float32),
            pltpu.VMEM((chunks, self.pair, self.latent), jnp.bfloat16),
            pltpu.VMEM((chunks, self.rope, self.pair), jnp.bfloat16),
            pltpu.VMEM((chunks, self.rows, self.pair), jnp.float32),
            pltpu.VMEM((self.rows, self.pair), jnp.float32),
            pltpu.VMEM((self.rows, self.latent), jnp.float32),
            pltpu.VMEM((self.rows, self.latent), jnp.bfloat16),
            DMA((self.steps + 3,)),
            DMA((self.most,)),
            DMA((self.most, 4)),
        ]


def own_queries(q_lat, q_rope, fresh):
    def copies(plan, qbuf, qrbuf, newraw, sem):
        steps, heads = plan.steps, plan.heads
        out = [
            pltpu.make_async_copy(q_lat.at[t], qbuf.at[pl.ds(t * heads, heads)], sem.at[t])
            for t in range(steps)
        ]
        out.append(pltpu.make_async_copy(q_rope, qrbuf, sem.at[steps]))
        out.append(pltpu.make_async_copy(fresh, newraw, sem.at[steps + 1]))
        return out

    return copies


def visiting_queries(payload):
    def copies(plan, qbuf, qrbuf, newraw, sem):
        rows, heads = plan.rows, plan.heads
        out = [
            pltpu.make_async_copy(
                payload.at[pl.ds(rows, plan.rope), pl.ds(t * heads, heads)], qrbuf.at[t], sem.at[t]
            )
            for t in range(plan.steps)
        ]
        out.append(pltpu.make_async_copy(payload.at[pl.ds(0, rows)], qbuf, sem.at[plan.steps]))
        out.append(
            pltpu.make_async_copy(payload.at[pl.ds(rows + plan.rope, 16)], newraw, sem.at[plan.steps + 1])
        )
        return out

    return copies


def attention(plan, scr, queries, block_copies, count, limit, marked, out_copy):
    (qbuf, qrbuf, qrt, newraw, newpad, kbuf, rbuf, sbuf, mbuf, acc, obuf, qsem, ksem, rsem) = scr
    steps, heads, latent, pair = plan.steps, plan.heads, plan.latent, plan.pair
    copies = queries(plan, qbuf, qrbuf, newraw, qsem)
    for copy in copies:
        copy.start()
    chunks = ceil_div(count, 2)

    def each(j, what):
        block_copies(j, jnp.minimum(j, count - 1), what, kbuf, rbuf, ksem, rsem)

    def launch(j, carry):
        each(j, lambda copy: copy.start())
        return carry

    lax.fori_loop(0, 2 * chunks, launch, 0)
    for copy in copies:
        copy.wait()
    for t in range(steps):
        qrt[pl.ds(t * heads, heads), :] = qrbuf[t].astype(jnp.float32).T.astype(jnp.bfloat16)
    newpad[...] = jnp.zeros_like(newpad)
    if plan.visitor:
        newpad[0:steps, :latent] = newraw[...].astype(jnp.float32)[0:steps]
        newpad[0:steps, latent:] = newraw[...].astype(jnp.float32)[8 : 8 + steps, : plan.rope]
    else:
        newpad[0:steps, :] = newraw[...].astype(jnp.float32)
    new_lat = newpad[:, :latent].astype(jnp.bfloat16)
    new_rope = newpad[:, latent:].astype(jnp.bfloat16)
    fresh_scores = (contract_last(qbuf[...], new_lat) + contract_last(qrt[...], new_rope)) * SCALE
    step_of = lax.broadcasted_iota(jnp.int32, (plan.rows, plan.block), 0) // heads
    new_of = lax.broadcasted_iota(jnp.int32, (plan.rows, plan.block), 1)
    fresh_scores = jnp.where(new_of <= step_of, fresh_scores, -jnp.inf)
    mbuf[...] = jnp.full_like(mbuf, -jnp.inf)

    def score(c, carry):
        each(2 * c, lambda copy: copy.wait())
        each(2 * c + 1, lambda copy: copy.wait())
        rope = rbuf[c]
        s = contract_last(qbuf[...], kbuf[c]) + jnp.dot(
            qrt[...], rope, preferred_element_type=jnp.float32
        )
        usable = lax.broadcasted_iota(jnp.int32, (1, pair), 1) + c * pair < limit
        if marked:
            usable = usable & (rope[0:1, :].astype(jnp.float32) < LIMIT)
        s = jnp.where(usable, s * SCALE, -jnp.inf)
        sbuf[c] = s
        mbuf[...] = jnp.maximum(mbuf[...], s)
        return carry

    lax.fori_loop(0, chunks, score, 0)
    highest = jnp.maximum(
        jnp.max(mbuf[...], axis=1, keepdims=True), jnp.max(fresh_scores, axis=1, keepdims=True)
    )
    new_w = jnp.exp(fresh_scores - highest)
    new_sum = jnp.sum(new_w, axis=1, keepdims=True)
    acc[...] = jnp.dot(new_w.astype(jnp.bfloat16), new_lat, preferred_element_type=jnp.float32)
    mbuf[...] = jnp.zeros_like(mbuf)

    def weigh(c, carry):
        w = jnp.exp(sbuf[c] - highest)
        mbuf[...] += w
        acc[...] += jnp.dot(w.astype(jnp.bfloat16), kbuf[c], preferred_element_type=jnp.float32)
        return carry

    lax.fori_loop(0, chunks, weigh, 0)
    total = new_sum + jnp.sum(mbuf[...], axis=1, keepdims=True)
    obuf[...] = (acc[...] / total).astype(jnp.bfloat16)
    outs = [out_copy(t, obuf.at[pl.ds(t * heads, heads)], qsem.at[t]) for t in range(steps)]
    for copy in outs:
        copy.start()
    for copy in outs:
        copy.wait()


def plain_copies(lat, rope, pick, block):
    def copies(source, j, kbuf, rbuf, ksem, rsem):
        b = pick(source)
        c, side = j // 2, pl.multiple_of((j % 2) * block, block)
        return [
            pltpu.make_async_copy(lat.at[b], kbuf.at[c, pl.ds(side, block)], ksem.at[j]),
            pltpu.make_async_copy(rope.at[b], rbuf.at[c, :, pl.ds(side, block)], rsem.at[j, 0]),
        ]

    return copies


def every(copies):
    def each(j, source, what, *bufs):
        for copy in copies(source, j, *bufs):
            what(copy)

    return each


def packed_copies(got, pick, block, rope_rows, latent):
    parts = latent // block

    def copies(source, j, kbuf, rbuf, ksem, rsem):
        e = pick(source)
        c, side = j // 2, pl.multiple_of((j % 2) * block, block)
        out = [
            pltpu.make_async_copy(
                got.at[e, pl.ds(0, block)], kbuf.at[c, pl.ds(side, block)], ksem.at[j]
            )
        ]
        for g in range(parts):
            out.append(
                pltpu.make_async_copy(
                    got.at[e, pl.ds(block, rope_rows), pl.ds(g * block, block)],
                    rbuf.at[c, pl.ds(g * rope_rows, rope_rows), pl.ds(side, block)],
                    rsem.at[j, g],
                )
            )
        return out

    return copies


def chunk_spans(blocks):
    sizes = []
    while blocks > 0:
        sizes.append(min(3 if not sizes or blocks == 3 else 2, blocks))
        blocks -= sizes[-1]
    return sizes


def cost(plan):
    keys = plan.most * plan.block
    return pl.CostEstimate(
        flops=2 * plan.rows * keys * (2 * plan.latent + plan.rope) // 2,
        bytes_accessed=2 * keys * (plan.latent + plan.rope) // 2,
        transcendentals=plan.rows * keys // 2,
    )


def resident_kernel(plan, slot, table, length, q_lat, q_rope, fresh, lat, rope, out, *scr):
    used = length[0]
    attention(
        plan, scr, own_queries(q_lat.at[slot], q_rope.at[slot], fresh.at[slot]),
        every(plain_copies(lat, rope, lambda j: table[0, j], plan.block)),
        ceil_div(used, plan.block), used, False,
        lambda t, src, sem: pltpu.make_async_copy(src, out.at[t], sem),
    )


def chunked(plan, sizes, chunks):
    rope_rows = plan.rope * plan.block // plan.latent
    starts = [sum(sizes[:i]) for i in range(len(sizes))]

    def each(j, source, what, *bufs):
        for ref, first, size in zip(chunks, starts, sizes, strict=True):

            @pl.when((source >= first) & (source < first + size))
            def _(ref=ref, first=first):
                for copy in packed_copies(ref, lambda e: e - first, plan.block, rope_rows, plan.latent)(source, j, *bufs):
                    what(copy)

    if len(sizes) == 1:
        return every(packed_copies(chunks[0], lambda e: e, plan.block, rope_rows, plan.latent))
    return each


def migrated_kernel(plan, slot, sizes, length, q_lat, q_rope, fresh, *refs):
    chunks, out, scr = refs[: len(sizes)], refs[len(sizes)], refs[len(sizes) + 1 :]
    used = length[0]
    attention(
        plan, scr, own_queries(q_lat.at[slot], q_rope.at[slot], fresh.at[slot]), chunked(plan, sizes, chunks),
        ceil_div(used, plan.block), used, False,
        lambda t, src, sem: pltpu.make_async_copy(src, out.at[t], sem),
    )


def visited_kernel(plan, sizes, length, payload, *refs):
    chunks, out, scr = refs[: len(sizes)], refs[len(sizes)], refs[len(sizes) + 1 :]
    used = length[0]
    attention(
        plan, scr, visiting_queries(payload), chunked(plan, sizes, chunks),
        ceil_div(used, plan.block), used, False,
        lambda t, src, sem: pltpu.make_async_copy(src, out.at[t], sem),
    )


def arriving_kernel(plan, slot, side, index, arrived, q_lat, q_rope, fresh, near, far, ready, moved, out, rbuf, rsem, *scr):
    sources = (ready, moved)
    pulls = [pltpu.make_async_copy(ref, rbuf.at[i], rsem.at[i]) for i, ref in enumerate(sources)]
    puts = [pltpu.make_async_copy(rbuf.at[i], out.at[slot - 1 + 2 * i], rsem.at[i]) for i in range(2)]
    for pull in pulls:
        pull.start()
    used = arrived[0]
    half = near.shape[0]
    rope_rows = plan.rope * plan.block // plan.latent

    def each(j, source, what, *bufs):
        s = index[source]
        for ref, here in ((near, True), (far, False)):

            @pl.when((s // half == side[0]) == here)
            def _(ref=ref):
                for copy in packed_copies(ref, lambda e: e, plan.block, rope_rows, plan.latent)(lax.rem(s, half), j, *bufs):
                    what(copy)

    for pull, put in zip(pulls, puts, strict=True):
        pull.wait()
        put.start()
    attention(
        plan, scr, own_queries(q_lat.at[slot], q_rope.at[slot], fresh.at[slot]), each,
        used, used * plan.block, True,
        lambda t, src, sem: pltpu.make_async_copy(src, out.at[slot, t], sem),
    )
    for put in puts:
        put.wait()


def pack_kernel(side, table, fill, lat, rope, out, lbuf, rbuf, pbuf, lsem, rsem, osem):
    blocks, block, latent = lat.shape
    home = side[0] * out.shape[0]
    rows = pbuf.shape[1]
    small = pltpu.make_async_copy(rope, rbuf, rsem)
    pulls = [pltpu.make_async_copy(lat.at[b], lbuf.at[b], lsem.at[b]) for b in range(blocks)]
    small.start()
    for pull in pulls:
        pull.start()
    small.wait()
    first = lax.broadcasted_iota(jnp.int32, rope.shape[1:], 0) == 0
    token = lax.broadcasted_iota(jnp.int32, rope.shape[1:], 1)
    for b in range(blocks):
        marked = jnp.where(first & (token >= fill[b]), MARK, rbuf[b].astype(jnp.float32)).astype(jnp.bfloat16)
        for g in range(latent // block):
            pbuf[b, :, g * block : (g + 1) * block] = marked[g * rows : (g + 1) * rows]
    for pull in pulls:
        pull.wait()

    def each(o, what):
        b = table[home + o]

        @pl.when(b >= 0)
        def _():
            for copy in (
                pltpu.make_async_copy(lbuf.at[b], out.at[o, pl.ds(0, block)], osem.at[b, 0]),
                pltpu.make_async_copy(pbuf.at[b], out.at[o, pl.ds(block, rows)], osem.at[b, 1]),
            ):
                what(copy)

    def launch(o, carry):
        each(o, lambda copy: copy.start())
        return carry

    def settle(o, carry):
        each(o, lambda copy: copy.wait())
        return carry

    lax.fori_loop(0, out.shape[0], launch, 0)
    lax.fori_loop(0, out.shape[0], settle, 0)


def fill_rows(fill, b, unit):
    return ceil_div(fill[b], unit) * unit


def plan_kernel(ends, side, table, fill, info, out):
    count, blocks = table.shape[0], fill.shape[0]
    half = count // 2
    unit = 16

    def add(o, totals):
        mine, theirs = totals
        b = table[(1 - side[0]) * half + o]
        mine += jnp.where(b >= 0, unit + fill_rows(fill, jnp.maximum(b, 0), unit), 0)
        b = info[side[0] * half + o]
        theirs += jnp.where(b >= 0, unit + ceil_div(info[count + jnp.maximum(b, 0)], unit) * unit, 0)
        return mine, theirs

    mine, theirs = lax.fori_loop(0, half, add, (jnp.int32(0), jnp.int32(0)))
    longest = jnp.maximum(mine, theirs)
    level = jnp.int32(0)
    for end in ends[:-1]:
        level += (longest > end).astype(jnp.int32)
    out[0] = level
    del blocks


def send_kernel(side, table, fill, lat, rope, out, lbuf, rbuf, buf, lsem, rsem, osem):
    blocks, block, latent = lat.shape
    half = table.shape[0] // 2
    unit = 16
    small = pltpu.make_async_copy(rope, rbuf, rsem)
    small.start()
    big = pltpu.make_async_copy(lat, lbuf, lsem)
    big.start()
    small.wait()
    big.wait()
    first = lax.broadcasted_iota(jnp.int32, rope.shape[1:], 0) == 0
    token = lax.broadcasted_iota(jnp.int32, rope.shape[1:], 1)

    def place(o, at):
        b = table[(1 - side[0]) * half + o]

        @pl.when(b >= 0)
        def _():
            start = pl.multiple_of(at, unit)
            marked = jnp.where(first & (token >= fill[b]), MARK, rbuf[b].astype(jnp.float32)).astype(jnp.bfloat16)
            for g in range(latent // block):
                buf[pl.ds(start, unit), g * block : (g + 1) * block] = marked[g * unit : (g + 1) * unit]

            def move(u, carry):
                row = pl.multiple_of(u * unit, unit)
                buf[pl.ds(pl.multiple_of(at + unit + row, unit), unit), :] = lbuf[b, pl.ds(row, unit), :]
                return carry

            lax.fori_loop(0, ceil_div(fill[b], unit), move, 0)

        return at + jnp.where(b >= 0, unit + fill_rows(fill, jnp.maximum(b, 0), unit), 0)

    lax.fori_loop(0, half, place, jnp.int32(0))
    put = pltpu.make_async_copy(buf, out, osem)
    put.start()
    put.wait()


def relay_kernel(side, info, got, out, buf, stage, sem, osem):
    blocks, tall, latent = stage.shape
    half = out.shape[0]
    count = 2 * half
    unit = 16
    pull = pltpu.make_async_copy(got, buf, sem)
    pull.start()
    pull.wait()

    def place(o, state):
        at, i = state
        b = info[side[0] * half + o]
        filled = ceil_div(info[count + jnp.maximum(b, 0)], unit)

        @pl.when(b >= 0)
        def _():
            block = tall - unit
            stage[i, pl.ds(block, unit), :] = buf[pl.ds(pl.multiple_of(at, unit), unit), :]

            def move(u, carry):
                row = pl.multiple_of(u * unit, unit)
                stage[i, pl.ds(row, unit), :] = buf[pl.ds(pl.multiple_of(at + unit + row, unit), unit), :]
                return carry

            def clear(u, carry):
                row = pl.multiple_of(u * unit, unit)
                stage[i, pl.ds(row, unit), :] = jnp.zeros((unit, latent), jnp.bfloat16)
                return carry

            lax.fori_loop(0, filled, move, 0)
            lax.fori_loop(filled, block // unit, clear, 0)
            pltpu.make_async_copy(stage.at[i], out.at[o], osem.at[i]).start()

        used = (b >= 0).astype(jnp.int32)
        return at + used * unit * (1 + filled), i + used

    def settle(o, i):
        b = info[side[0] * half + o]

        @pl.when(b >= 0)
        def _():
            pltpu.make_async_copy(stage.at[i], out.at[o], osem.at[i]).wait()

        return i + (b >= 0).astype(jnp.int32)

    lax.fori_loop(0, half, place, (jnp.int32(0), jnp.int32(0)))
    lax.fori_loop(0, half, settle, jnp.int32(0))


def chunk_kernel(spans, slot, lat, rope, q_lat, q_rope, fresh, *refs):
    outs, payload = refs[: len(spans)], refs[len(spans)]
    lbuf, rbuf, pbuf, qbuf, qrbuf, fbuf, mbuf, sem, osem, qsem = refs[len(spans) + 1 :]
    blocks, block, latent = lat.shape
    steps, heads = qbuf.shape[0] // block, block
    rows = pbuf.shape[1]
    wide = steps * heads
    pulls = [
        pltpu.make_async_copy(rope, rbuf, sem.at[0]),
        pltpu.make_async_copy(q_rope.at[slot], qrbuf, sem.at[1]),
        pltpu.make_async_copy(fresh.at[slot], fbuf, sem.at[2]),
        pltpu.make_async_copy(lat, lbuf, sem.at[3]),
    ]
    pulls += [
        pltpu.make_async_copy(q_lat.at[slot, t], qbuf.at[pl.ds(t * heads, heads)], sem.at[4 + t])
        for t in range(steps)
    ]
    for pull in pulls:
        pull.start()
    for pull in pulls:
        pull.wait()
    for b in range(blocks):
        for g in range(latent // block):
            pbuf[b, :, g * block : (g + 1) * block] = rbuf[b, g * rows : (g + 1) * rows]
    puts = []
    for i, ((first, size), out) in enumerate(zip(spans, outs, strict=True)):
        span = pl.ds(first, size)
        puts.append(pltpu.make_async_copy(lbuf.at[span], out.at[:, pl.ds(0, block)], osem.at[i, 0]))
        puts.append(pltpu.make_async_copy(pbuf.at[span], out.at[:, pl.ds(block, rows)], osem.at[i, 1]))
    mbuf[...] = jnp.zeros_like(mbuf)
    new = fbuf[...].astype(jnp.float32)
    mbuf[0:steps, :] = new[:, :latent]
    mbuf[8 : 8 + steps, : new.shape[1] - latent] = new[:, latent:]
    tail = qrbuf.shape[1]
    qbuf[wide + tail : wide + tail + 16, :] = mbuf[...].astype(jnp.bfloat16)
    for t in range(steps):
        qbuf[wide : wide + tail, t * heads : (t + 1) * heads] = qrbuf[t]
    puts.append(pltpu.make_async_copy(qbuf, payload, qsem))
    for put in puts:
        put.start()
    for put in puts:
        put.wait()


def shards(
    res_lat, res_rope, res_table, res_len, out_lat, out_rope, out_fill, send_table, arr_index,
    arr_count, mig_lat, mig_rope, mig_len, mig_bit, q_lat, q_rope, new_kv,
):
    count = lax.axis_size("dp")
    bits = count.bit_length() - 1
    slots, steps, heads, latent = q_lat.shape
    rope = q_rope.shape[2]
    block = res_lat.shape[1]
    requests = res_len.shape[0]
    assert requests == 1 and send_table.shape[0] == count
    make = functools.partial(Plan, steps=steps, heads=heads, latent=latent, rope=rope, block=block)
    rows = rope * block // latent
    blocks = out_lat.shape[0]

    half = count // 2
    far = bits - 1
    tall = block + rows
    side = (lax.axis_index("dp") >= half).astype(jnp.int32).reshape(1)
    groups = [list(range(half)), list(range(half, count))]

    def swapper(bit):
        route = [(i, i ^ 1 << bit) for i in range(count)]
        return lambda x: lax.ppermute(x, "dp", route)

    def within(x):
        return lax.all_to_all(x, "dp", split_axis=0, concat_axis=0, axis_index_groups=groups, tiled=True)

    info = swapper(far)(jnp.concatenate([send_table, out_fill, mig_len]))
    packed = pl.pallas_call(
        pack_kernel,
        out_shape=jax.ShapeDtypeStruct((half, tall, latent), jnp.bfloat16),
        in_specs=[SMEM, SMEM, SMEM, ANY, ANY],
        out_specs=ANY,
        scratch_shapes=[
            pltpu.VMEM((blocks, block, latent), jnp.bfloat16),
            pltpu.VMEM((blocks, rope, block), jnp.bfloat16),
            pltpu.VMEM((blocks, rows, latent), jnp.bfloat16),
            DMA((blocks,)), DMA, DMA((blocks, 2)),
        ],
        name="pack",
    )(side, send_table, out_fill, out_lat, out_rope)
    info, packed = lax.optimization_barrier((info, packed))
    near = within(packed)

    spans_far = [n for n in (256, 384, 512, 640, 768) if n < blocks * tall] + [blocks * tall]
    level = pl.pallas_call(
        functools.partial(plan_kernel, spans_far),
        out_shape=jax.ShapeDtypeStruct((1,), jnp.int32),
        in_specs=[SMEM] * 4,
        out_specs=SMEM,
        name="plan",
    )(side, send_table, out_fill, info)

    held = mig_lat.shape[0]
    sizes = chunk_spans(held)
    spans = [(sum(sizes[:i]), n) for i, n in enumerate(sizes)]
    mail = steps * heads + rope + 16

    def relay(size):
        def branch(side, table, fill, info, out_lat, out_rope, res, mig, queries):
            sent = pl.pallas_call(
                send_kernel,
                out_shape=jax.ShapeDtypeStruct((size, latent), jnp.bfloat16),
                in_specs=[SMEM, SMEM, SMEM, ANY, ANY],
                out_specs=ANY,
                scratch_shapes=[
                    pltpu.VMEM((blocks, block, latent), jnp.bfloat16),
                    pltpu.VMEM((blocks, rope, block), jnp.bfloat16),
                    pltpu.VMEM((size, latent), jnp.bfloat16),
                    DMA, DMA, DMA,
                ],
                name="send",
            )(side, table, fill, out_lat, out_rope)
            received = swapper(far)(sent)
            res_table, res_len, res_lat, res_rope = res
            sent, res_table, mig = lax.optimization_barrier((sent, res_table, mig))
            plan = make(res_table.shape[1])
            ready = pl.pallas_call(
                functools.partial(resident_kernel, plan, 0),
                out_shape=jax.ShapeDtypeStruct((steps, heads, latent), jnp.bfloat16),
                in_specs=[SMEM, SMEM, ANY, ANY, ANY, ANY, ANY],
                out_specs=ANY,
                scratch_shapes=plan.scratch(),
                cost_estimate=cost(plan),
                name="resident",
            )(res_table, res_len, *queries, res_lat, res_rope)
            *chunks, payload = pl.pallas_call(
                functools.partial(chunk_kernel, spans, requests + 1),
                out_shape=[jax.ShapeDtypeStruct((n, tall, latent), jnp.bfloat16) for n in sizes]
                + [jax.ShapeDtypeStruct((mail, latent), jnp.bfloat16)],
                in_specs=[ANY] * 5,
                out_specs=[ANY] * (len(sizes) + 1),
                scratch_shapes=[
                    pltpu.VMEM((held, block, latent), jnp.bfloat16),
                    pltpu.VMEM((held, rope, block), jnp.bfloat16),
                    pltpu.VMEM((held, rows, latent), jnp.bfloat16),
                    pltpu.VMEM((mail, latent), jnp.bfloat16),
                    pltpu.VMEM((steps, rope, heads), jnp.bfloat16),
                    pltpu.VMEM(new_kv.shape[1:], jnp.bfloat16),
                    pltpu.VMEM((16, latent), jnp.float32),
                    DMA((4 + steps,)), DMA((len(sizes), 2)), DMA,
                ],
                cost_estimate=pl.CostEstimate(flops=0, bytes_accessed=8 << 20, transcendentals=0),
                name="chunk",
            )(*mig, *queries)
            relayed = pl.pallas_call(
                relay_kernel,
                out_shape=jax.ShapeDtypeStruct((half, tall, latent), jnp.bfloat16),
                in_specs=[SMEM, SMEM, ANY],
                out_specs=ANY,
                scratch_shapes=[
                    pltpu.VMEM((size, latent), jnp.bfloat16),
                    pltpu.VMEM((blocks, tall, latent), jnp.bfloat16),
                    DMA, DMA((blocks,)),
                ],
                name="relay",
            )(side, info, received)
            return relayed, ready, chunks, payload

        return branch

    queries = (q_lat, q_rope, new_kv)
    relayed, ready, chunks, payload = lax.switch(
        level[0],
        [relay(size) for size in spans_far],
        side, send_table, out_fill, info, out_lat, out_rope,
        (res_table, res_len, res_lat, res_rope), (mig_lat, mig_rope), queries,
    )
    relayed, near = lax.optimization_barrier((relayed, near))
    distant = within(relayed)

    ends = [sum(sizes[: i + 1]) * block for i in range(len(sizes))]

    def migrate(length, chunks, queries):
        plan = make(held)
        return pl.pallas_call(
            functools.partial(migrated_kernel, plan, requests + 1, sizes),
            out_shape=jax.ShapeDtypeStruct((steps, heads, latent), jnp.bfloat16),
            in_specs=[SMEM] + [ANY] * (3 + len(sizes)),
            out_specs=ANY,
            scratch_shapes=plan.scratch(),
            cost_estimate=cost(plan),
            name="migrated",
        )(length, *queries, *chunks)

    def ship(swap, own, other, chunks, most):
        longest = jnp.maximum(own, other)[0]
        level = sum((longest > end).astype(jnp.int32) for end in ends[: most - 1])

        def sending(k):
            return lambda chunks: [swap(x) if i <= k else x for i, x in enumerate(chunks)]

        return lax.switch(level, [sending(k) for k in range(most)], chunks)

    def stay(own, other, chunks, payload, queries):
        return migrate(own, chunks, queries)

    def near_partner(bit):
        swap = swapper(bit)

        def branch(own, other, chunks, payload, queries):
            other = swap(own)
            return migrate(other, ship(swap, own, other, chunks, len(sizes)), queries)

        return branch

    most = max(1, len(sizes) - 2)

    def far_partner(own, other, chunks, payload, queries):
        swap = swapper(far)

        def short(own, other, chunks, payload, queries):
            return migrate(other, ship(swap, own, other, chunks, most), queries)

        def long(own, other, chunks, payload, queries):
            plan = make(held, visitor=True)
            result = pl.pallas_call(
                functools.partial(visited_kernel, plan, sizes),
                out_shape=jax.ShapeDtypeStruct((steps, heads, latent), jnp.bfloat16),
                in_specs=[SMEM] + [ANY] * (1 + len(sizes)),
                out_specs=ANY,
                scratch_shapes=plan.scratch(),
                cost_estimate=cost(plan),
                name="visited",
            )(own, swap(payload), *chunks)
            return swap(result)

        longest = jnp.maximum(own, other)[0]
        return lax.cond(longest > ends[most - 1], long, short, own, other, chunks, payload, queries)

    moved = lax.switch(
        mig_bit[0] + 1,
        [stay] + [near_partner(bit) for bit in range(far)] + [far_partner],
        mig_len, info[count + blocks :], chunks, payload, queries,
    )

    plan = make(arr_index.shape[0])
    return pl.pallas_call(
        functools.partial(arriving_kernel, plan, requests),
        out_shape=jax.ShapeDtypeStruct((slots, steps, heads, latent), jnp.bfloat16),
        in_specs=[SMEM, SMEM, SMEM] + [ANY] * 7,
        out_specs=ANY,
        scratch_shapes=[pltpu.VMEM((2, steps, heads, latent), jnp.bfloat16), DMA((2,))] + plan.scratch(),
        cost_estimate=cost(plan),
        name="arriving",
    )(side, arr_index, arr_count, *queries, near, distant, ready, moved)


def solution(mesh):
    whole = P(("groups", "dp"))
    return jax.shard_map(shards, mesh=mesh, in_specs=(whole,) * 17, out_specs=whole, check_vma=False)
```

```python
import functools

import jax
import jax.numpy as jnp
from jax import lax
from jax.experimental import pallas as pl
from jax.experimental.pallas import tpu as pltpu
from jax.sharding import PartitionSpec as P

SCALE = 192.0 ** (-0.5)
MARK = 1e30
LIMIT = 1e20
ANY = pl.BlockSpec(memory_space=pl.ANY)
SMEM = pl.BlockSpec(memory_space=pltpu.SMEM)
DMA = pltpu.SemaphoreType.DMA


def contract_last(a, b):
    return lax.dot_general(a, b, (((1,), (1,)), ((), ())), preferred_element_type=jnp.float32)


def ceil_div(a, b):
    return (a + b - 1) // b


class Plan:
    def __init__(self, most, steps, heads, latent, rope, block, visitor=False):
        self.visitor = visitor
        self.most = most + most % 2
        self.steps, self.heads, self.latent, self.rope, self.block = steps, heads, latent, rope, block
        self.rows = steps * heads
        self.pair = 2 * block

    def scratch(self):
        chunks = self.most // 2
        return [
            pltpu.VMEM((self.rows, self.latent), jnp.bfloat16),
            pltpu.VMEM((self.steps, self.rope, self.heads), jnp.bfloat16),
            pltpu.VMEM((self.rows, self.rope), jnp.bfloat16),
            pltpu.VMEM((16, self.latent) if self.visitor else (self.steps, self.latent + self.rope), jnp.bfloat16),
            pltpu.VMEM((self.block, self.latent + self.rope), jnp.float32),
            pltpu.VMEM((chunks, self.pair, self.latent), jnp.bfloat16),
            pltpu.VMEM((chunks, self.rope, self.pair), jnp.bfloat16),
            pltpu.VMEM((chunks, self.rows, self.pair), jnp.float32),
            pltpu.VMEM((self.rows, self.pair), jnp.float32),
            pltpu.VMEM((self.rows, self.latent), jnp.float32),
            pltpu.VMEM((self.rows, self.latent), jnp.bfloat16),
            DMA((self.steps + 3,)),
            DMA((self.most,)),
            DMA((self.most, 4)),
        ]


def own_queries(q_lat, q_rope, fresh):
    def copies(plan, qbuf, qrbuf, newraw, sem):
        steps, heads = plan.steps, plan.heads
        out = [
            pltpu.make_async_copy(q_lat.at[t], qbuf.at[pl.ds(t * heads, heads)], sem.at[t])
            for t in range(steps)
        ]
        out.append(pltpu.make_async_copy(q_rope, qrbuf, sem.at[steps]))
        out.append(pltpu.make_async_copy(fresh, newraw, sem.at[steps + 1]))
        return out

    return copies


def visiting_queries(payload):
    def copies(plan, qbuf, qrbuf, newraw, sem):
        rows, heads = plan.rows, plan.heads
        out = [
            pltpu.make_async_copy(
                payload.at[pl.ds(rows, plan.rope), pl.ds(t * heads, heads)], qrbuf.at[t], sem.at[t]
            )
            for t in range(plan.steps)
        ]
        out.append(pltpu.make_async_copy(payload.at[pl.ds(0, rows)], qbuf, sem.at[plan.steps]))
        out.append(
            pltpu.make_async_copy(payload.at[pl.ds(rows + plan.rope, 16)], newraw, sem.at[plan.steps + 1])
        )
        return out

    return copies


def attention(plan, scr, queries, block_copies, count, limit, marked, out_copy):
    (qbuf, qrbuf, qrt, newraw, newpad, kbuf, rbuf, sbuf, mbuf, acc, obuf, qsem, ksem, rsem) = scr
    steps, heads, latent, pair = plan.steps, plan.heads, plan.latent, plan.pair
    copies = queries(plan, qbuf, qrbuf, newraw, qsem)
    for copy in copies:
        copy.start()
    chunks = ceil_div(count, 2)

    def each(j, what):
        block_copies(j, jnp.minimum(j, count - 1), what, kbuf, rbuf, ksem, rsem)

    def launch(j, carry):
        each(j, lambda copy: copy.start())
        return carry

    lax.fori_loop(0, 2 * chunks, launch, 0)
    for copy in copies:
        copy.wait()
    for t in range(steps):
        qrt[pl.ds(t * heads, heads), :] = qrbuf[t].astype(jnp.float32).T.astype(jnp.bfloat16)
    newpad[...] = jnp.zeros_like(newpad)
    if plan.visitor:
        newpad[0:steps, :latent] = newraw[...].astype(jnp.float32)[0:steps]
        newpad[0:steps, latent:] = newraw[...].astype(jnp.float32)[8 : 8 + steps, : plan.rope]
    else:
        newpad[0:steps, :] = newraw[...].astype(jnp.float32)
    new_lat = newpad[:, :latent].astype(jnp.bfloat16)
    new_rope = newpad[:, latent:].astype(jnp.bfloat16)
    fresh_scores = (contract_last(qbuf[...], new_lat) + contract_last(qrt[...], new_rope)) * SCALE
    step_of = lax.broadcasted_iota(jnp.int32, (plan.rows, plan.block), 0) // heads
    new_of = lax.broadcasted_iota(jnp.int32, (plan.rows, plan.block), 1)
    fresh_scores = jnp.where(new_of <= step_of, fresh_scores, -jnp.inf)
    mbuf[...] = jnp.full_like(mbuf, -jnp.inf)

    def score(c, carry):
        each(2 * c, lambda copy: copy.wait())
        each(2 * c + 1, lambda copy: copy.wait())
        rope = rbuf[c]
        s = contract_last(qbuf[...], kbuf[c]) + jnp.dot(
            qrt[...], rope, preferred_element_type=jnp.float32
        )
        usable = lax.broadcasted_iota(jnp.int32, (1, pair), 1) + c * pair < limit
        if marked:
            usable = usable & (rope[0:1, :].astype(jnp.float32) < LIMIT)
        s = jnp.where(usable, s * SCALE, -jnp.inf)
        sbuf[c] = s
        mbuf[...] = jnp.maximum(mbuf[...], s)
        return carry

    lax.fori_loop(0, chunks, score, 0)
    highest = jnp.maximum(
        jnp.max(mbuf[...], axis=1, keepdims=True), jnp.max(fresh_scores, axis=1, keepdims=True)
    )
    new_w = jnp.exp(fresh_scores - highest)
    new_sum = jnp.sum(new_w, axis=1, keepdims=True)
    acc[...] = jnp.dot(new_w.astype(jnp.bfloat16), new_lat, preferred_element_type=jnp.float32)
    mbuf[...] = jnp.zeros_like(mbuf)

    def weigh(c, carry):
        w = jnp.exp(sbuf[c] - highest)
        mbuf[...] += w
        acc[...] += jnp.dot(w.astype(jnp.bfloat16), kbuf[c], preferred_element_type=jnp.float32)
        return carry

    lax.fori_loop(0, chunks, weigh, 0)
    total = new_sum + jnp.sum(mbuf[...], axis=1, keepdims=True)
    obuf[...] = (acc[...] / total).astype(jnp.bfloat16)
    outs = [out_copy(t, obuf.at[pl.ds(t * heads, heads)], qsem.at[t]) for t in range(steps)]
    for copy in outs:
        copy.start()
    for copy in outs:
        copy.wait()


def plain_copies(lat, rope, pick, block):
    def copies(source, j, kbuf, rbuf, ksem, rsem):
        b = pick(source)
        c, side = j // 2, pl.multiple_of((j % 2) * block, block)
        return [
            pltpu.make_async_copy(lat.at[b], kbuf.at[c, pl.ds(side, block)], ksem.at[j]),
            pltpu.make_async_copy(rope.at[b], rbuf.at[c, :, pl.ds(side, block)], rsem.at[j, 0]),
        ]

    return copies


def every(copies):
    def each(j, source, what, *bufs):
        for copy in copies(source, j, *bufs):
            what(copy)

    return each


def packed_copies(got, pick, block, rope_rows, latent):
    parts = latent // block

    def copies(source, j, kbuf, rbuf, ksem, rsem):
        e = pick(source)
        c, side = j // 2, pl.multiple_of((j % 2) * block, block)
        out = [
            pltpu.make_async_copy(
                got.at[e, pl.ds(0, block)], kbuf.at[c, pl.ds(side, block)], ksem.at[j]
            )
        ]
        for g in range(parts):
            out.append(
                pltpu.make_async_copy(
                    got.at[e, pl.ds(block, rope_rows), pl.ds(g * block, block)],
                    rbuf.at[c, pl.ds(g * rope_rows, rope_rows), pl.ds(side, block)],
                    rsem.at[j, g],
                )
            )
        return out

    return copies


def chunk_spans(blocks):
    sizes = []
    while blocks > 0:
        sizes.append(min(3 if not sizes or blocks == 3 else 2, blocks))
        blocks -= sizes[-1]
    return sizes


def cost(plan):
    keys = plan.most * plan.block
    return pl.CostEstimate(
        flops=2 * plan.rows * keys * (2 * plan.latent + plan.rope) // 2,
        bytes_accessed=2 * keys * (plan.latent + plan.rope) // 2,
        transcendentals=plan.rows * keys // 2,
    )


def resident_kernel(plan, slot, table, length, q_lat, q_rope, fresh, lat, rope, out, *scr):
    used = length[0]
    attention(
        plan, scr, own_queries(q_lat.at[slot], q_rope.at[slot], fresh.at[slot]),
        every(plain_copies(lat, rope, lambda j: table[0, j], plan.block)),
        ceil_div(used, plan.block), used, False,
        lambda t, src, sem: pltpu.make_async_copy(src, out.at[t], sem),
    )


def chunked(plan, sizes, chunks):
    rope_rows = plan.rope * plan.block // plan.latent
    starts = [sum(sizes[:i]) for i in range(len(sizes))]

    def each(j, source, what, *bufs):
        for ref, first, size in zip(chunks, starts, sizes, strict=True):

            @pl.when((source >= first) & (source < first + size))
            def _(ref=ref, first=first):
                for copy in packed_copies(ref, lambda e: e - first, plan.block, rope_rows, plan.latent)(source, j, *bufs):
                    what(copy)

    if len(sizes) == 1:
        return every(packed_copies(chunks[0], lambda e: e, plan.block, rope_rows, plan.latent))
    return each


def migrated_kernel(plan, slot, sizes, length, q_lat, q_rope, fresh, *refs):
    chunks, out, scr = refs[: len(sizes)], refs[len(sizes) + 1], refs[len(sizes) + 2 :]
    used = length[0]
    attention(
        plan, scr, own_queries(q_lat.at[slot], q_rope.at[slot], fresh.at[slot]), chunked(plan, sizes, chunks),
        ceil_div(used, plan.block), used, False,
        lambda t, src, sem: pltpu.make_async_copy(src, out.at[slot, t], sem),
    )


def visited_kernel(plan, sizes, length, payload, *refs):
    chunks, out, scr = refs[: len(sizes)], refs[len(sizes)], refs[len(sizes) + 1 :]
    used = length[0]
    attention(
        plan, scr, visiting_queries(payload), chunked(plan, sizes, chunks),
        ceil_div(used, plan.block), used, False,
        lambda t, src, sem: pltpu.make_async_copy(src, out.at[t], sem),
    )


def place_kernel(slot, back, base, out, buf, sem):
    del base
    for copy in (pltpu.make_async_copy(back, buf, sem.at[0]), pltpu.make_async_copy(buf, out.at[slot], sem.at[1])):
        copy.start()
        copy.wait()


def arriving_kernel(plan, slot, index, arrived, q_lat, q_rope, fresh, got, ready, out, rbuf, rsem, *scr):
    fetch = pltpu.make_async_copy(ready, rbuf, rsem.at[0])
    fetch.start()
    used = arrived[0]
    fetch.wait()
    put = pltpu.make_async_copy(rbuf, out.at[slot - 1], rsem.at[1])
    put.start()
    attention(
        plan, scr, own_queries(q_lat.at[slot], q_rope.at[slot], fresh.at[slot]),
        every(packed_copies(got, lambda j: index[j], plan.block, plan.rope * plan.block // plan.latent, plan.latent)),
        used, used * plan.block, True,
        lambda t, src, sem: pltpu.make_async_copy(src, out.at[slot, t], sem),
    )
    put.wait()


def pack_kernel(table, fill, lat, rope, out, lbuf, rbuf, pbuf, lsem, rsem, osem):
    blocks, block, latent = lat.shape
    rows = pbuf.shape[1]
    small = pltpu.make_async_copy(rope, rbuf, rsem)
    pulls = [pltpu.make_async_copy(lat.at[b], lbuf.at[b], lsem.at[b]) for b in range(blocks)]
    small.start()
    for pull in pulls:
        pull.start()
    small.wait()
    first = lax.broadcasted_iota(jnp.int32, rope.shape[1:], 0) == 0
    token = lax.broadcasted_iota(jnp.int32, rope.shape[1:], 1)
    for b in range(blocks):
        marked = jnp.where(first & (token >= fill[b]), MARK, rbuf[b].astype(jnp.float32)).astype(jnp.bfloat16)
        for g in range(latent // block):
            pbuf[b, :, g * block : (g + 1) * block] = marked[g * rows : (g + 1) * rows]
    for pull in pulls:
        pull.wait()

    def each(o, what):
        b = table[o]

        @pl.when(b >= 0)
        def _():
            for copy in (
                pltpu.make_async_copy(lbuf.at[b], out.at[o, pl.ds(0, block)], osem.at[b, 0]),
                pltpu.make_async_copy(pbuf.at[b], out.at[o, pl.ds(block, rows)], osem.at[b, 1]),
            ):
                what(copy)

    def launch(o, carry):
        each(o, lambda copy: copy.start())
        return carry

    def settle(o, carry):
        each(o, lambda copy: copy.wait())
        return carry

    lax.fori_loop(0, out.shape[0], launch, 0)
    lax.fori_loop(0, out.shape[0], settle, 0)


def chunk_kernel(spans, slot, lat, rope, q_lat, q_rope, fresh, *refs):
    outs, payload = refs[: len(spans)], refs[len(spans)]
    lbuf, rbuf, pbuf, qbuf, qrbuf, fbuf, mbuf, sem, osem, qsem = refs[len(spans) + 1 :]
    blocks, block, latent = lat.shape
    steps, heads = qbuf.shape[0] // block, block
    rows = pbuf.shape[1]
    wide = steps * heads
    pulls = [
        pltpu.make_async_copy(rope, rbuf, sem.at[0]),
        pltpu.make_async_copy(q_rope.at[slot], qrbuf, sem.at[1]),
        pltpu.make_async_copy(fresh.at[slot], fbuf, sem.at[2]),
        pltpu.make_async_copy(lat, lbuf, sem.at[3]),
    ]
    pulls += [
        pltpu.make_async_copy(q_lat.at[slot, t], qbuf.at[pl.ds(t * heads, heads)], sem.at[4 + t])
        for t in range(steps)
    ]
    for pull in pulls:
        pull.start()
    for pull in pulls:
        pull.wait()
    for b in range(blocks):
        for g in range(latent // block):
            pbuf[b, :, g * block : (g + 1) * block] = rbuf[b, g * rows : (g + 1) * rows]
    puts = []
    for i, ((first, size), out) in enumerate(zip(spans, outs, strict=True)):
        span = pl.ds(first, size)
        puts.append(pltpu.make_async_copy(lbuf.at[span], out.at[:, pl.ds(0, block)], osem.at[i, 0]))
        puts.append(pltpu.make_async_copy(pbuf.at[span], out.at[:, pl.ds(block, rows)], osem.at[i, 1]))
    mbuf[...] = jnp.zeros_like(mbuf)
    new = fbuf[...].astype(jnp.float32)
    mbuf[0:steps, :] = new[:, :latent]
    mbuf[8 : 8 + steps, : new.shape[1] - latent] = new[:, latent:]
    tail = qrbuf.shape[1]
    qbuf[wide + tail : wide + tail + 16, :] = mbuf[...].astype(jnp.bfloat16)
    for t in range(steps):
        qbuf[wide : wide + tail, t * heads : (t + 1) * heads] = qrbuf[t]
    puts.append(pltpu.make_async_copy(qbuf, payload, qsem))
    for put in puts:
        put.start()
    for put in puts:
        put.wait()


def shards(
    res_lat, res_rope, res_table, res_len, out_lat, out_rope, out_fill, send_table, arr_index,
    arr_count, mig_lat, mig_rope, mig_len, mig_bit, q_lat, q_rope, new_kv,
):
    count = lax.axis_size("dp")
    bits = count.bit_length() - 1
    slots, steps, heads, latent = q_lat.shape
    rope = q_rope.shape[2]
    block = res_lat.shape[1]
    requests = res_len.shape[0]
    assert requests == 1 and send_table.shape[0] == count
    make = functools.partial(Plan, steps=steps, heads=heads, latent=latent, rope=rope, block=block)
    rows = rope * block // latent
    blocks = out_lat.shape[0]

    packed = pl.pallas_call(
        pack_kernel,
        out_shape=jax.ShapeDtypeStruct((count, block + rows, latent), jnp.bfloat16),
        in_specs=[SMEM, SMEM, ANY, ANY],
        out_specs=ANY,
        scratch_shapes=[
            pltpu.VMEM((blocks, block, latent), jnp.bfloat16),
            pltpu.VMEM((blocks, rope, block), jnp.bfloat16),
            pltpu.VMEM((blocks, rows, latent), jnp.bfloat16),
            DMA((blocks,)), DMA, DMA((blocks, 2)),
        ],
        name="pack",
    )(send_table, out_fill, out_lat, out_rope)
    def swapper(bit):
        route = [(i, i ^ 1 << bit) for i in range(count)]
        return lambda x: lax.ppermute(x, "dp", route)

    far = bits - 1
    early = [swapper(bit)(mig_len) for bit in (far, far - 1)]
    packed, early = lax.optimization_barrier((packed, early))
    got = lax.all_to_all(packed, "dp", split_axis=0, concat_axis=0, tiled=True)

    plan = make(res_table.shape[1])
    res_table, packed = lax.optimization_barrier((res_table, packed))
    ready = pl.pallas_call(
        functools.partial(resident_kernel, plan, 0),
        out_shape=jax.ShapeDtypeStruct((steps, heads, latent), jnp.bfloat16),
        in_specs=[SMEM, SMEM, ANY, ANY, ANY, ANY, ANY],
        out_specs=ANY,
        scratch_shapes=plan.scratch(),
        cost_estimate=cost(plan),
        name="resident",
    )(res_table, res_len, q_lat, q_rope, new_kv, res_lat, res_rope)

    held = mig_lat.shape[0]
    sizes = chunk_spans(held)
    levels = [n for n in (2, 4, 6, 8) if n < held]
    mig_lat, mig_rope, packed = lax.optimization_barrier((mig_lat, mig_rope, packed))
    spans = [(sum(sizes[:i]), n) for i, n in enumerate(sizes)] + [(0, n) for n in levels]
    mail = steps * heads + rope + 16
    *pieces, payload = pl.pallas_call(
        functools.partial(chunk_kernel, spans, requests + 1),
        out_shape=[jax.ShapeDtypeStruct((n, block + rows, latent), jnp.bfloat16) for _, n in spans]
        + [jax.ShapeDtypeStruct((mail, latent), jnp.bfloat16)],
        in_specs=[ANY] * 5,
        out_specs=[ANY] * (len(spans) + 1),
        scratch_shapes=[
            pltpu.VMEM((held, block, latent), jnp.bfloat16),
            pltpu.VMEM((held, rope, block), jnp.bfloat16),
            pltpu.VMEM((held, rows, latent), jnp.bfloat16),
            pltpu.VMEM((mail, latent), jnp.bfloat16),
            pltpu.VMEM((steps, rope, heads), jnp.bfloat16),
            pltpu.VMEM(new_kv.shape[1:], jnp.bfloat16),
            pltpu.VMEM((16, latent), jnp.float32),
            DMA((4 + steps,)), DMA((len(spans), 2)), DMA,
        ],
        name="chunk",
    )(mig_lat, mig_rope, q_lat, q_rope, new_kv)
    chunks, prefixes = pieces[: len(sizes)], pieces[len(sizes) :]
    ready, chunks = lax.optimization_barrier((ready, chunks))

    ends = [sum(sizes[: i + 1]) * block for i in range(len(sizes))]

    def level_of(one, other):
        longest = jnp.maximum(one, other)[0]
        return sum((longest > end).astype(jnp.int32) for end in ends[:-1])

    def near(bit):
        swap = swapper(bit)

        def branch(length, early, chunks, payload):
            other = early[1] if bit == far - 1 else swap(length)

            def sending(k):
                return lambda chunks: [swap(x) if i <= k else x for i, x in enumerate(chunks)]

            level = level_of(length, other)
            chunks = lax.switch(level, [sending(k) for k in range(len(sizes))], chunks)
            return other, chunks, payload

        return branch

    limit = levels[-1] * block if levels else 0

    def distant(length, early, chunks, payload):
        longest = jnp.maximum(length, early[0])[0]
        payload = lax.cond(longest > limit, swapper(far), lambda x: x, payload)
        return early[0], chunks, payload

    length, chunks, payload = lax.switch(
        mig_bit[0] + 1,
        [lambda length, early, chunks, payload: (length, chunks, payload)]
        + [near(bit) for bit in range(far)]
        + [distant],
        mig_len, early, chunks, payload,
    )

    whole = jax.ShapeDtypeStruct((slots, steps, heads, latent), jnp.bfloat16)

    def arrive(index, arrived, got, ready, q_lat, q_rope, new_kv):
        plan = make(index.shape[0])
        return pl.pallas_call(
            functools.partial(arriving_kernel, plan, requests),
            out_shape=whole,
            in_specs=[SMEM, SMEM, ANY, ANY, ANY, ANY, ANY],
            out_specs=ANY,
            scratch_shapes=[pltpu.VMEM((steps, heads, latent), jnp.bfloat16), DMA((2,))] + plan.scratch(),
            cost_estimate=cost(plan),
            name="arriving",
        )(index, arrived, q_lat, q_rope, new_kv, got, ready)

    def migrate(length, q_lat, q_rope, new_kv, sizes, chunks, base):
        plan = make(sum(sizes))
        return pl.pallas_call(
            functools.partial(migrated_kernel, plan, requests + 1, sizes),
            out_shape=whole,
            in_specs=[SMEM] + [ANY] * (4 + len(sizes)),
            out_specs=ANY,
            scratch_shapes=plan.scratch(),
            input_output_aliases={4 + len(sizes): 0},
            cost_estimate=cost(plan),
            name="migrated",
        )(length, q_lat, q_rope, new_kv, *chunks, base)

    swap = swapper(far)

    def local(arrival, queries, own, length, chunks, prefixes, payload):
        base = arrive(*arrival, *queries)
        return migrate(length, *queries, sizes, chunks, base)

    def shipped(k):
        def branch(arrival, queries, own, length, chunks, prefixes, payload):
            cache = swap(prefixes[k])
            base = arrive(*arrival, *queries)
            return migrate(length, *queries, [levels[k]], [cache], base)

        return branch

    def visited(arrival, queries, own, length, chunks, prefixes, payload):
        plan = make(held, visitor=True)
        result = pl.pallas_call(
            functools.partial(visited_kernel, plan, sizes),
            out_shape=jax.ShapeDtypeStruct((steps, heads, latent), jnp.bfloat16),
            in_specs=[SMEM] + [ANY] * (1 + len(sizes)),
            out_specs=ANY,
            scratch_shapes=plan.scratch(),
            cost_estimate=cost(plan),
            name="visited",
        )(own, payload, *chunks)
        back = swap(result)
        base = arrive(*arrival, *queries)
        return pl.pallas_call(
            functools.partial(place_kernel, requests + 1),
            out_shape=whole,
            in_specs=[ANY, ANY],
            out_specs=ANY,
            scratch_shapes=[pltpu.VMEM((steps, heads, latent), jnp.bfloat16), DMA((2,))],
            input_output_aliases={1: 0},
            name="place",
        )(back, base)

    longest = jnp.maximum(mig_len, length)[0]
    step = 1 + sum((longest > n * block).astype(jnp.int32) for n in levels)
    return lax.switch(
        jnp.where(mig_bit[0] == far, step, 0),
        [local] + [shipped(k) for k in range(len(levels))] + [visited],
        (arr_index, arr_count, got, ready), (q_lat, q_rope, new_kv), mig_len, length, chunks, prefixes, payload,
    )


def solution(mesh):
    whole = P(("groups", "dp"))
    return jax.shard_map(shards, mesh=mesh, in_specs=(whole,) * 17, out_specs=whole, check_vma=False)
```

```python
import functools

import jax
import jax.numpy as jnp
from jax import lax
from jax.experimental import pallas as pl
from jax.experimental.pallas import tpu as pltpu
from jax.sharding import PartitionSpec as P

SCALE = 192.0 ** (-0.5)
MARK = 1e30
LIMIT = 1e20
ANY = pl.BlockSpec(memory_space=pl.ANY)
SMEM = pl.BlockSpec(memory_space=pltpu.SMEM)
DMA = pltpu.SemaphoreType.DMA


def contract_last(a, b):
    return lax.dot_general(a, b, (((1,), (1,)), ((), ())), preferred_element_type=jnp.float32)


def ceil_div(a, b):
    return (a + b - 1) // b


class Plan:
    def __init__(self, most, steps, heads, latent, rope, block, visitor=False):
        self.visitor = visitor
        self.most = most + most % 2
        self.steps, self.heads, self.latent, self.rope, self.block = steps, heads, latent, rope, block
        self.rows = steps * heads
        self.pair = 2 * block

    def scratch(self):
        chunks = self.most // 2
        return [
            pltpu.VMEM((self.rows, self.latent), jnp.bfloat16),
            pltpu.VMEM((self.steps, self.rope, self.heads), jnp.bfloat16),
            pltpu.VMEM((self.rows, self.rope), jnp.bfloat16),
            pltpu.VMEM((16, self.latent) if self.visitor else (self.steps, self.latent + self.rope), jnp.bfloat16),
            pltpu.VMEM((self.block, self.latent + self.rope), jnp.float32),
            pltpu.VMEM((chunks, self.pair, self.latent), jnp.bfloat16),
            pltpu.VMEM((chunks, self.rope, self.pair), jnp.bfloat16),
            pltpu.VMEM((chunks, self.rows, self.pair), jnp.float32),
            pltpu.VMEM((self.rows, self.pair), jnp.float32),
            pltpu.VMEM((self.rows, self.latent), jnp.float32),
            pltpu.VMEM((self.rows, self.latent), jnp.bfloat16),
            DMA((self.steps + 3,)),
            DMA((self.most,)),
            DMA((self.most, 4)),
        ]


def own_queries(q_lat, q_rope, fresh):
    def copies(plan, qbuf, qrbuf, newraw, sem):
        steps, heads = plan.steps, plan.heads
        out = [
            pltpu.make_async_copy(q_lat.at[t], qbuf.at[pl.ds(t * heads, heads)], sem.at[t])
            for t in range(steps)
        ]
        out.append(pltpu.make_async_copy(q_rope, qrbuf, sem.at[steps]))
        out.append(pltpu.make_async_copy(fresh, newraw, sem.at[steps + 1]))
        return out

    return copies


def visiting_queries(payload):
    def copies(plan, qbuf, qrbuf, newraw, sem):
        rows, heads = plan.rows, plan.heads
        out = [
            pltpu.make_async_copy(
                payload.at[pl.ds(rows, plan.rope), pl.ds(t * heads, heads)], qrbuf.at[t], sem.at[t]
            )
            for t in range(plan.steps)
        ]
        out.append(pltpu.make_async_copy(payload.at[pl.ds(0, rows)], qbuf, sem.at[plan.steps]))
        out.append(
            pltpu.make_async_copy(payload.at[pl.ds(rows + plan.rope, 16)], newraw, sem.at[plan.steps + 1])
        )
        return out

    return copies


def attention(plan, scr, queries, block_copies, count, limit, marked, out_copy):
    (qbuf, qrbuf, qrt, newraw, newpad, kbuf, rbuf, sbuf, mbuf, acc, obuf, qsem, ksem, rsem) = scr
    steps, heads, latent, pair = plan.steps, plan.heads, plan.latent, plan.pair
    copies = queries(plan, qbuf, qrbuf, newraw, qsem)
    for copy in copies:
        copy.start()
    chunks = ceil_div(count, 2)

    def each(j, what):
        block_copies(j, jnp.minimum(j, count - 1), what, kbuf, rbuf, ksem, rsem)

    def launch(j, carry):
        each(j, lambda copy: copy.start())
        return carry

    lax.fori_loop(0, 2 * chunks, launch, 0)
    for copy in copies:
        copy.wait()
    for t in range(steps):
        qrt[pl.ds(t * heads, heads), :] = qrbuf[t].astype(jnp.float32).T.astype(jnp.bfloat16)
    newpad[...] = jnp.zeros_like(newpad)
    if plan.visitor:
        newpad[0:steps, :latent] = newraw[...].astype(jnp.float32)[0:steps]
        newpad[0:steps, latent:] = newraw[...].astype(jnp.float32)[8 : 8 + steps, : plan.rope]
    else:
        newpad[0:steps, :] = newraw[...].astype(jnp.float32)
    new_lat = newpad[:, :latent].astype(jnp.bfloat16)
    new_rope = newpad[:, latent:].astype(jnp.bfloat16)
    fresh_scores = (contract_last(qbuf[...], new_lat) + contract_last(qrt[...], new_rope)) * SCALE
    step_of = lax.broadcasted_iota(jnp.int32, (plan.rows, plan.block), 0) // heads
    new_of = lax.broadcasted_iota(jnp.int32, (plan.rows, plan.block), 1)
    fresh_scores = jnp.where(new_of <= step_of, fresh_scores, -jnp.inf)
    mbuf[...] = jnp.full_like(mbuf, -jnp.inf)

    def score(c, carry):
        each(2 * c, lambda copy: copy.wait())
        each(2 * c + 1, lambda copy: copy.wait())
        rope = rbuf[c]
        s = contract_last(qbuf[...], kbuf[c]) + jnp.dot(
            qrt[...], rope, preferred_element_type=jnp.float32
        )
        usable = lax.broadcasted_iota(jnp.int32, (1, pair), 1) + c * pair < limit
        if marked:
            usable = usable & (rope[0:1, :].astype(jnp.float32) < LIMIT)
        s = jnp.where(usable, s * SCALE, -jnp.inf)
        sbuf[c] = s
        mbuf[...] = jnp.maximum(mbuf[...], s)
        return carry

    lax.fori_loop(0, chunks, score, 0)
    highest = jnp.maximum(
        jnp.max(mbuf[...], axis=1, keepdims=True), jnp.max(fresh_scores, axis=1, keepdims=True)
    )
    new_w = jnp.exp(fresh_scores - highest)
    new_sum = jnp.sum(new_w, axis=1, keepdims=True)
    acc[...] = jnp.dot(new_w.astype(jnp.bfloat16), new_lat, preferred_element_type=jnp.float32)
    mbuf[...] = jnp.zeros_like(mbuf)

    def weigh(c, carry):
        w = jnp.exp(sbuf[c] - highest)
        mbuf[...] += w
        acc[...] += jnp.dot(w.astype(jnp.bfloat16), kbuf[c], preferred_element_type=jnp.float32)
        return carry

    lax.fori_loop(0, chunks, weigh, 0)
    total = new_sum + jnp.sum(mbuf[...], axis=1, keepdims=True)
    obuf[...] = (acc[...] / total).astype(jnp.bfloat16)
    outs = [out_copy(t, obuf.at[pl.ds(t * heads, heads)], qsem.at[t]) for t in range(steps)]
    for copy in outs:
        copy.start()
    for copy in outs:
        copy.wait()


def plain_copies(lat, rope, pick, block):
    def copies(source, j, kbuf, rbuf, ksem, rsem):
        b = pick(source)
        c, side = j // 2, pl.multiple_of((j % 2) * block, block)
        return [
            pltpu.make_async_copy(lat.at[b], kbuf.at[c, pl.ds(side, block)], ksem.at[j]),
            pltpu.make_async_copy(rope.at[b], rbuf.at[c, :, pl.ds(side, block)], rsem.at[j, 0]),
        ]

    return copies


def every(copies):
    def each(j, source, what, *bufs):
        for copy in copies(source, j, *bufs):
            what(copy)

    return each


def packed_copies(got, pick, block, rope_rows, latent):
    parts = latent // block

    def copies(source, j, kbuf, rbuf, ksem, rsem):
        e = pick(source)
        c, side = j // 2, pl.multiple_of((j % 2) * block, block)
        out = [
            pltpu.make_async_copy(
                got.at[e, pl.ds(0, block)], kbuf.at[c, pl.ds(side, block)], ksem.at[j]
            )
        ]
        for g in range(parts):
            out.append(
                pltpu.make_async_copy(
                    got.at[e, pl.ds(block, rope_rows), pl.ds(g * block, block)],
                    rbuf.at[c, pl.ds(g * rope_rows, rope_rows), pl.ds(side, block)],
                    rsem.at[j, g],
                )
            )
        return out

    return copies


def chunk_spans(blocks):
    sizes = []
    while blocks > 0:
        sizes.append(min(3 if not sizes or blocks == 3 else 2, blocks))
        blocks -= sizes[-1]
    return sizes


def cost(plan):
    keys = plan.most * plan.block
    return pl.CostEstimate(
        flops=2 * plan.rows * keys * (2 * plan.latent + plan.rope) // 2,
        bytes_accessed=2 * keys * (plan.latent + plan.rope) // 2,
        transcendentals=plan.rows * keys // 2,
    )


def resident_kernel(plan, slot, table, length, q_lat, q_rope, fresh, lat, rope, out, *scr):
    used = length[0]
    attention(
        plan, scr, own_queries(q_lat.at[slot], q_rope.at[slot], fresh.at[slot]),
        every(plain_copies(lat, rope, lambda j: table[0, j], plan.block)),
        ceil_div(used, plan.block), used, False,
        lambda t, src, sem: pltpu.make_async_copy(src, out.at[t], sem),
    )


def chunked(plan, sizes, chunks):
    rope_rows = plan.rope * plan.block // plan.latent
    starts = [sum(sizes[:i]) for i in range(len(sizes))]

    def each(j, source, what, *bufs):
        for ref, first, size in zip(chunks, starts, sizes, strict=True):

            @pl.when((source >= first) & (source < first + size))
            def _(ref=ref, first=first):
                for copy in packed_copies(ref, lambda e: e - first, plan.block, rope_rows, plan.latent)(source, j, *bufs):
                    what(copy)

    if len(sizes) == 1:
        return every(packed_copies(chunks[0], lambda e: e, plan.block, rope_rows, plan.latent))
    return each


def migrated_kernel(plan, slot, sizes, length, q_lat, q_rope, fresh, *refs):
    chunks, out, scr = refs[: len(sizes)], refs[len(sizes) + 1], refs[len(sizes) + 2 :]
    used = length[0]
    attention(
        plan, scr, own_queries(q_lat.at[slot], q_rope.at[slot], fresh.at[slot]), chunked(plan, sizes, chunks),
        ceil_div(used, plan.block), used, False,
        lambda t, src, sem: pltpu.make_async_copy(src, out.at[slot, t], sem),
    )


def visited_kernel(plan, sizes, length, payload, *refs):
    chunks, out, scr = refs[: len(sizes)], refs[len(sizes)], refs[len(sizes) + 1 :]
    used = length[0]
    attention(
        plan, scr, visiting_queries(payload), chunked(plan, sizes, chunks),
        ceil_div(used, plan.block), used, False,
        lambda t, src, sem: pltpu.make_async_copy(src, out.at[t], sem),
    )


def place_kernel(slot, back, base, out, buf, sem):
    del base
    for copy in (pltpu.make_async_copy(back, buf, sem.at[0]), pltpu.make_async_copy(buf, out.at[slot], sem.at[1])):
        copy.start()
        copy.wait()


def arriving_kernel(plan, slot, index, arrived, q_lat, q_rope, fresh, got, ready, out, rbuf, rsem, *scr):
    fetch = pltpu.make_async_copy(ready, rbuf, rsem.at[0])
    fetch.start()
    used = arrived[0]
    fetch.wait()
    put = pltpu.make_async_copy(rbuf, out.at[slot - 1], rsem.at[1])
    put.start()
    attention(
        plan, scr, own_queries(q_lat.at[slot], q_rope.at[slot], fresh.at[slot]),
        every(packed_copies(got, lambda j: index[j], plan.block, plan.rope * plan.block // plan.latent, plan.latent)),
        used, used * plan.block, True,
        lambda t, src, sem: pltpu.make_async_copy(src, out.at[slot, t], sem),
    )
    put.wait()


def pack_kernel(table, fill, lat, rope, out, lbuf, rbuf, pbuf, lsem, rsem, osem):
    blocks, block, latent = lat.shape
    rows = pbuf.shape[1]
    small = pltpu.make_async_copy(rope, rbuf, rsem)
    pulls = [pltpu.make_async_copy(lat.at[b], lbuf.at[b], lsem.at[b]) for b in range(blocks)]
    small.start()
    for pull in pulls:
        pull.start()
    def each(o, what, src, span, i):
        b = table[o]

        @pl.when(b >= 0)
        def _():
            what(pltpu.make_async_copy(src.at[b], out.at[o, span], osem.at[b, i]))

    top, tail = (lbuf, pl.ds(0, block), 0), (pbuf, pl.ds(block, rows), 1)

    def launch(part):
        def body(o, carry):
            each(o, lambda copy: copy.start(), *part)
            return carry

        lax.fori_loop(0, out.shape[0], body, 0)

    for pull in pulls:
        pull.wait()
    launch(top)
    small.wait()
    first = lax.broadcasted_iota(jnp.int32, rope.shape[1:], 0) == 0
    token = lax.broadcasted_iota(jnp.int32, rope.shape[1:], 1)
    for b in range(blocks):
        marked = jnp.where(first & (token >= fill[b]), MARK, rbuf[b].astype(jnp.float32)).astype(jnp.bfloat16)
        for g in range(latent // block):
            pbuf[b, :, g * block : (g + 1) * block] = marked[g * rows : (g + 1) * rows]
    launch(tail)

    def settle(o, carry):
        each(o, lambda copy: copy.wait(), *top)
        each(o, lambda copy: copy.wait(), *tail)
        return carry

    lax.fori_loop(0, out.shape[0], settle, 0)


def chunk_kernel(spans, slot, lat, rope, q_lat, q_rope, fresh, *refs):
    outs, payload = refs[: len(spans)], refs[len(spans)]
    lbuf, rbuf, pbuf, qbuf, qrbuf, fbuf, mbuf, sem, osem, qsem = refs[len(spans) + 1 :]
    blocks, block, latent = lat.shape
    steps, heads = qbuf.shape[0] // block, block
    rows = pbuf.shape[1]
    wide = steps * heads
    pulls = [
        pltpu.make_async_copy(rope, rbuf, sem.at[0]),
        pltpu.make_async_copy(q_rope.at[slot], qrbuf, sem.at[1]),
        pltpu.make_async_copy(fresh.at[slot], fbuf, sem.at[2]),
        pltpu.make_async_copy(lat, lbuf, sem.at[3]),
    ]
    pulls += [
        pltpu.make_async_copy(q_lat.at[slot, t], qbuf.at[pl.ds(t * heads, heads)], sem.at[4 + t])
        for t in range(steps)
    ]
    for pull in pulls:
        pull.start()
    for pull in pulls:
        pull.wait()
    for b in range(blocks):
        for g in range(latent // block):
            pbuf[b, :, g * block : (g + 1) * block] = rbuf[b, g * rows : (g + 1) * rows]
    puts = []
    for i, ((first, size), out) in enumerate(zip(spans, outs, strict=True)):
        span = pl.ds(first, size)
        puts.append(pltpu.make_async_copy(lbuf.at[span], out.at[:, pl.ds(0, block)], osem.at[i, 0]))
        puts.append(pltpu.make_async_copy(pbuf.at[span], out.at[:, pl.ds(block, rows)], osem.at[i, 1]))
    mbuf[...] = jnp.zeros_like(mbuf)
    new = fbuf[...].astype(jnp.float32)
    mbuf[0:steps, :] = new[:, :latent]
    mbuf[8 : 8 + steps, : new.shape[1] - latent] = new[:, latent:]
    tail = qrbuf.shape[1]
    qbuf[wide + tail : wide + tail + 16, :] = mbuf[...].astype(jnp.bfloat16)
    for t in range(steps):
        qbuf[wide : wide + tail, t * heads : (t + 1) * heads] = qrbuf[t]
    puts.append(pltpu.make_async_copy(qbuf, payload, qsem))
    for put in puts:
        put.start()
    for put in puts:
        put.wait()


def shards(
    res_lat, res_rope, res_table, res_len, out_lat, out_rope, out_fill, send_table, arr_index,
    arr_count, mig_lat, mig_rope, mig_len, mig_bit, q_lat, q_rope, new_kv,
):
    count = lax.axis_size("dp")
    bits = count.bit_length() - 1
    slots, steps, heads, latent = q_lat.shape
    rope = q_rope.shape[2]
    block = res_lat.shape[1]
    requests = res_len.shape[0]
    assert requests == 1 and send_table.shape[0] == count
    make = functools.partial(Plan, steps=steps, heads=heads, latent=latent, rope=rope, block=block)
    rows = rope * block // latent
    blocks = out_lat.shape[0]

    def pack(table, fill, lat, rot):
        return pl.pallas_call(
            pack_kernel,
            out_shape=jax.ShapeDtypeStruct((count, block + rows, latent), jnp.bfloat16),
            in_specs=[SMEM, SMEM, ANY, ANY],
            out_specs=ANY,
            scratch_shapes=[
                pltpu.VMEM((blocks, block, latent), jnp.bfloat16),
                pltpu.VMEM((blocks, rope, block), jnp.bfloat16),
                pltpu.VMEM((blocks, rows, latent), jnp.bfloat16),
                DMA((blocks,)), DMA, DMA((blocks, 2)),
            ],
            cost_estimate=pl.CostEstimate(flops=0, bytes_accessed=8 << 20, transcendentals=0),
            name="pack",
        )(table, fill, lat, rot)

    def swapper(bit):
        route = [(i, i ^ 1 << bit) for i in range(count)]
        return lambda x: lax.ppermute(x, "dp", route)

    def opening(bit):
        return lambda length, *blocks: (swapper(bit)(length), pack(*blocks))

    far = bits - 1
    early, packed = lax.switch(
        mig_bit[0] + 1,
        [lambda length, *blocks: (length, pack(*blocks))] + [opening(bit) for bit in range(bits)],
        mig_len, send_table, out_fill, out_lat, out_rope,
    )
    got = lax.all_to_all(packed, "dp", split_axis=0, concat_axis=0, tiled=True)

    plan = make(res_table.shape[1])
    res_table, packed = lax.optimization_barrier((res_table, packed))
    ready = pl.pallas_call(
        functools.partial(resident_kernel, plan, 0),
        out_shape=jax.ShapeDtypeStruct((steps, heads, latent), jnp.bfloat16),
        in_specs=[SMEM, SMEM, ANY, ANY, ANY, ANY, ANY],
        out_specs=ANY,
        scratch_shapes=plan.scratch(),
        cost_estimate=cost(plan),
        name="resident",
    )(res_table, res_len, q_lat, q_rope, new_kv, res_lat, res_rope)

    held = mig_lat.shape[0]
    sizes = chunk_spans(held)
    levels = [n for n in (2, 4, 6, 8) if n < held]
    mig_lat, mig_rope, packed = lax.optimization_barrier((mig_lat, mig_rope, packed))
    spans = [(sum(sizes[:i]), n) for i, n in enumerate(sizes)] + [(0, n) for n in levels]
    mail = steps * heads + rope + 16
    *pieces, payload = pl.pallas_call(
        functools.partial(chunk_kernel, spans, requests + 1),
        out_shape=[jax.ShapeDtypeStruct((n, block + rows, latent), jnp.bfloat16) for _, n in spans]
        + [jax.ShapeDtypeStruct((mail, latent), jnp.bfloat16)],
        in_specs=[ANY] * 5,
        out_specs=[ANY] * (len(spans) + 1),
        scratch_shapes=[
            pltpu.VMEM((held, block, latent), jnp.bfloat16),
            pltpu.VMEM((held, rope, block), jnp.bfloat16),
            pltpu.VMEM((held, rows, latent), jnp.bfloat16),
            pltpu.VMEM((mail, latent), jnp.bfloat16),
            pltpu.VMEM((steps, rope, heads), jnp.bfloat16),
            pltpu.VMEM(new_kv.shape[1:], jnp.bfloat16),
            pltpu.VMEM((16, latent), jnp.float32),
            DMA((4 + steps,)), DMA((len(spans), 2)), DMA,
        ],
        name="chunk",
    )(mig_lat, mig_rope, q_lat, q_rope, new_kv)
    chunks, prefixes = pieces[: len(sizes)], pieces[len(sizes) :]
    ready, chunks = lax.optimization_barrier((ready, chunks))

    ends = [sum(sizes[: i + 1]) * block for i in range(len(sizes))]

    def level_of(one, other):
        longest = jnp.maximum(one, other)[0]
        return sum((longest > end).astype(jnp.int32) for end in ends[:-1])

    def near(bit):
        swap = swapper(bit)

        def branch(length, early, chunks, payload):
            other = early

            def sending(k):
                return lambda chunks: [swap(x) if i <= k else x for i, x in enumerate(chunks)]

            level = level_of(length, other)
            chunks = lax.switch(level, [sending(k) for k in range(len(sizes))], chunks)
            return other, chunks, payload

        return branch

    limit = levels[-1] * block if levels else 0

    def distant(length, early, chunks, payload):
        longest = jnp.maximum(length, early)[0]
        payload = lax.cond(longest > limit, swapper(far), lambda x: x, payload)
        return early, chunks, payload

    length, chunks, payload = lax.switch(
        mig_bit[0] + 1,
        [lambda length, early, chunks, payload: (length, chunks, payload)]
        + [near(bit) for bit in range(far)]
        + [distant],
        mig_len, early, chunks, payload,
    )

    whole = jax.ShapeDtypeStruct((slots, steps, heads, latent), jnp.bfloat16)

    def arrive(index, arrived, got, ready, q_lat, q_rope, new_kv):
        plan = make(index.shape[0])
        return pl.pallas_call(
            functools.partial(arriving_kernel, plan, requests),
            out_shape=whole,
            in_specs=[SMEM, SMEM, ANY, ANY, ANY, ANY, ANY],
            out_specs=ANY,
            scratch_shapes=[pltpu.VMEM((steps, heads, latent), jnp.bfloat16), DMA((2,))] + plan.scratch(),
            cost_estimate=cost(plan),
            name="arriving",
        )(index, arrived, q_lat, q_rope, new_kv, got, ready)

    def migrate(length, q_lat, q_rope, new_kv, sizes, chunks, base):
        plan = make(sum(sizes))
        return pl.pallas_call(
            functools.partial(migrated_kernel, plan, requests + 1, sizes),
            out_shape=whole,
            in_specs=[SMEM] + [ANY] * (4 + len(sizes)),
            out_specs=ANY,
            scratch_shapes=plan.scratch(),
            input_output_aliases={4 + len(sizes): 0},
            cost_estimate=cost(plan),
            name="migrated",
        )(length, q_lat, q_rope, new_kv, *chunks, base)

    swap = swapper(far)

    def local(arrival, queries, own, length, chunks, prefixes, payload):
        base = arrive(*arrival, *queries)
        return migrate(length, *queries, sizes, chunks, base)

    def shipped(k):
        def branch(arrival, queries, own, length, chunks, prefixes, payload):
            cache = swap(prefixes[k])
            base = arrive(*arrival, *queries)
            return migrate(length, *queries, [levels[k]], [cache], base)

        return branch

    def visited(arrival, queries, own, length, chunks, prefixes, payload):
        plan = make(held, visitor=True)
        result = pl.pallas_call(
            functools.partial(visited_kernel, plan, sizes),
            out_shape=jax.ShapeDtypeStruct((steps, heads, latent), jnp.bfloat16),
            in_specs=[SMEM] + [ANY] * (1 + len(sizes)),
            out_specs=ANY,
            scratch_shapes=plan.scratch(),
            cost_estimate=cost(plan),
            name="visited",
        )(own, payload, *chunks)
        back = swap(result)
        base = arrive(*arrival, *queries)
        return pl.pallas_call(
            functools.partial(place_kernel, requests + 1),
            out_shape=whole,
            in_specs=[ANY, ANY],
            out_specs=ANY,
            scratch_shapes=[pltpu.VMEM((steps, heads, latent), jnp.bfloat16), DMA((2,))],
            input_output_aliases={1: 0},
            name="place",
        )(back, base)

    longest = jnp.maximum(mig_len, length)[0]
    step = 1 + sum((longest > n * block).astype(jnp.int32) for n in levels)
    return lax.switch(
        jnp.where(mig_bit[0] == far, step, 0),
        [local] + [shipped(k) for k in range(len(levels))] + [visited],
        (arr_index, arr_count, got, ready), (q_lat, q_rope, new_kv), mig_len, length, chunks, prefixes, payload,
    )


def solution(mesh):
    whole = P(("groups", "dp"))
    return jax.shard_map(shards, mesh=mesh, in_specs=(whole,) * 17, out_specs=whole, check_vma=False)
```

```python
import functools

import jax
import jax.numpy as jnp
from jax import lax
from jax.experimental import pallas as pl
from jax.experimental.pallas import tpu as pltpu
from jax.sharding import PartitionSpec as P

SCALE = 192.0 ** (-0.5)
MARK = 1e30
LIMIT = 1e20
ANY = pl.BlockSpec(memory_space=pl.ANY)
SMEM = pl.BlockSpec(memory_space=pltpu.SMEM)
DMA = pltpu.SemaphoreType.DMA


def contract_last(a, b):
    return lax.dot_general(a, b, (((1,), (1,)), ((), ())), preferred_element_type=jnp.float32)


def ceil_div(a, b):
    return (a + b - 1) // b


class Plan:
    def __init__(self, most, steps, heads, latent, rope, block, visitor=False):
        self.visitor = visitor
        self.most = most + most % 2
        self.steps, self.heads, self.latent, self.rope, self.block = steps, heads, latent, rope, block
        self.rows = steps * heads
        self.pair = 2 * block

    def scratch(self):
        chunks = self.most // 2
        return [
            pltpu.VMEM((self.rows, self.latent), jnp.bfloat16),
            pltpu.VMEM((self.steps, self.rope, self.heads), jnp.bfloat16),
            pltpu.VMEM((self.rows, self.rope), jnp.bfloat16),
            pltpu.VMEM((16, self.latent) if self.visitor else (self.steps, self.latent + self.rope), jnp.bfloat16),
            pltpu.VMEM((self.block, self.latent + self.rope), jnp.float32),
            pltpu.VMEM((chunks, self.pair, self.latent), jnp.bfloat16),
            pltpu.VMEM((chunks, self.rope, self.pair), jnp.bfloat16),
            pltpu.VMEM((chunks, self.rows, self.pair), jnp.float32),
            pltpu.VMEM((self.rows, self.pair), jnp.float32),
            pltpu.VMEM((self.rows, self.latent), jnp.float32),
            pltpu.VMEM((self.rows, self.latent), jnp.bfloat16),
            DMA((self.steps + 3,)),
            DMA((self.most,)),
            DMA((self.most, 4)),
        ]


def own_queries(q_lat, q_rope, fresh):
    def copies(plan, qbuf, qrbuf, newraw, sem):
        steps, heads = plan.steps, plan.heads
        out = [
            pltpu.make_async_copy(q_lat.at[t], qbuf.at[pl.ds(t * heads, heads)], sem.at[t])
            for t in range(steps)
        ]
        out.append(pltpu.make_async_copy(q_rope, qrbuf, sem.at[steps]))
        out.append(pltpu.make_async_copy(fresh, newraw, sem.at[steps + 1]))
        return out

    return copies


def visiting_queries(payload):
    def copies(plan, qbuf, qrbuf, newraw, sem):
        rows, heads = plan.rows, plan.heads
        out = [
            pltpu.make_async_copy(
                payload.at[pl.ds(rows, plan.rope), pl.ds(t * heads, heads)], qrbuf.at[t], sem.at[t]
            )
            for t in range(plan.steps)
        ]
        out.append(pltpu.make_async_copy(payload.at[pl.ds(0, rows)], qbuf, sem.at[plan.steps]))
        out.append(
            pltpu.make_async_copy(payload.at[pl.ds(rows + plan.rope, 16)], newraw, sem.at[plan.steps + 1])
        )
        return out

    return copies


def attention(plan, scr, queries, block_copies, count, limit, marked, out_copy):
    (qbuf, qrbuf, qrt, newraw, newpad, kbuf, rbuf, sbuf, mbuf, acc, obuf, qsem, ksem, rsem) = scr
    steps, heads, latent, pair = plan.steps, plan.heads, plan.latent, plan.pair
    copies = queries(plan, qbuf, qrbuf, newraw, qsem)
    for copy in copies:
        copy.start()
    chunks = ceil_div(count, 2)

    def each(j, what):
        block_copies(j, jnp.minimum(j, count - 1), what, kbuf, rbuf, ksem, rsem)

    def launch(j, carry):
        each(j, lambda copy: copy.start())
        return carry

    lax.fori_loop(0, 2 * chunks, launch, 0)
    for copy in copies:
        copy.wait()
    for t in range(steps):
        qrt[pl.ds(t * heads, heads), :] = qrbuf[t].astype(jnp.float32).T.astype(jnp.bfloat16)
    newpad[...] = jnp.zeros_like(newpad)
    if plan.visitor:
        newpad[0:steps, :latent] = newraw[...].astype(jnp.float32)[0:steps]
        newpad[0:steps, latent:] = newraw[...].astype(jnp.float32)[8 : 8 + steps, : plan.rope]
    else:
        newpad[0:steps, :] = newraw[...].astype(jnp.float32)
    new_lat = newpad[:, :latent].astype(jnp.bfloat16)
    new_rope = newpad[:, latent:].astype(jnp.bfloat16)
    fresh_scores = (contract_last(qbuf[...], new_lat) + contract_last(qrt[...], new_rope)) * SCALE
    step_of = lax.broadcasted_iota(jnp.int32, (plan.rows, plan.block), 0) // heads
    new_of = lax.broadcasted_iota(jnp.int32, (plan.rows, plan.block), 1)
    fresh_scores = jnp.where(new_of <= step_of, fresh_scores, -jnp.inf)
    mbuf[...] = jnp.full_like(mbuf, -jnp.inf)

    def score(c, carry):
        each(2 * c, lambda copy: copy.wait())
        each(2 * c + 1, lambda copy: copy.wait())
        rope = rbuf[c]
        s = contract_last(qbuf[...], kbuf[c]) + jnp.dot(
            qrt[...], rope, preferred_element_type=jnp.float32
        )
        usable = lax.broadcasted_iota(jnp.int32, (1, pair), 1) + c * pair < limit
        if marked:
            usable = usable & (rope[0:1, :].astype(jnp.float32) < LIMIT)
        s = jnp.where(usable, s * SCALE, -jnp.inf)
        sbuf[c] = s
        mbuf[...] = jnp.maximum(mbuf[...], s)
        return carry

    lax.fori_loop(0, chunks, score, 0)
    highest = jnp.maximum(
        jnp.max(mbuf[...], axis=1, keepdims=True), jnp.max(fresh_scores, axis=1, keepdims=True)
    )
    new_w = jnp.exp(fresh_scores - highest)
    new_sum = jnp.sum(new_w, axis=1, keepdims=True)
    acc[...] = jnp.dot(new_w.astype(jnp.bfloat16), new_lat, preferred_element_type=jnp.float32)
    mbuf[...] = jnp.zeros_like(mbuf)

    def weigh(c, carry):
        w = jnp.exp(sbuf[c] - highest)
        mbuf[...] += w
        acc[...] += jnp.dot(w.astype(jnp.bfloat16), kbuf[c], preferred_element_type=jnp.float32)
        return carry

    lax.fori_loop(0, chunks, weigh, 0)
    total = new_sum + jnp.sum(mbuf[...], axis=1, keepdims=True)
    obuf[...] = (acc[...] / total).astype(jnp.bfloat16)
    outs = [out_copy(t, obuf.at[pl.ds(t * heads, heads)], qsem.at[t]) for t in range(steps)]
    for copy in outs:
        copy.start()
    for copy in outs:
        copy.wait()


def plain_copies(lat, rope, pick, block):
    def copies(source, j, kbuf, rbuf, ksem, rsem):
        b = pick(source)
        c, side = j // 2, pl.multiple_of((j % 2) * block, block)
        return [
            pltpu.make_async_copy(lat.at[b], kbuf.at[c, pl.ds(side, block)], ksem.at[j]),
            pltpu.make_async_copy(rope.at[b], rbuf.at[c, :, pl.ds(side, block)], rsem.at[j, 0]),
        ]

    return copies


def every(copies):
    def each(j, source, what, *bufs):
        for copy in copies(source, j, *bufs):
            what(copy)

    return each


def packed_copies(got, pick, block, rope_rows, latent):
    parts = latent // block

    def copies(source, j, kbuf, rbuf, ksem, rsem):
        e = pick(source)
        c, side = j // 2, pl.multiple_of((j % 2) * block, block)
        out = [
            pltpu.make_async_copy(
                got.at[e, pl.ds(0, block)], kbuf.at[c, pl.ds(side, block)], ksem.at[j]
            )
        ]
        for g in range(parts):
            out.append(
                pltpu.make_async_copy(
                    got.at[e, pl.ds(block, rope_rows), pl.ds(g * block, block)],
                    rbuf.at[c, pl.ds(g * rope_rows, rope_rows), pl.ds(side, block)],
                    rsem.at[j, g],
                )
            )
        return out

    return copies


def chunk_spans(blocks):
    sizes = []
    while blocks > 0:
        sizes.append(min(3 if not sizes or blocks == 3 else 2, blocks))
        blocks -= sizes[-1]
    return sizes


def cost(plan):
    keys = plan.most * plan.block
    return pl.CostEstimate(
        flops=2 * plan.rows * keys * (2 * plan.latent + plan.rope) // 2,
        bytes_accessed=2 * keys * (plan.latent + plan.rope) // 2,
        transcendentals=plan.rows * keys // 2,
    )


def resident_kernel(plan, slot, table, length, q_lat, q_rope, fresh, lat, rope, out, *scr):
    used = length[0]
    attention(
        plan, scr, own_queries(q_lat.at[slot], q_rope.at[slot], fresh.at[slot]),
        every(plain_copies(lat, rope, lambda j: table[0, j], plan.block)),
        ceil_div(used, plan.block), used, False,
        lambda t, src, sem: pltpu.make_async_copy(src, out.at[t], sem),
    )


def chunked(plan, sizes, chunks):
    rope_rows = plan.rope * plan.block // plan.latent
    starts = [sum(sizes[:i]) for i in range(len(sizes))]

    def each(j, source, what, *bufs):
        for ref, first, size in zip(chunks, starts, sizes, strict=True):

            @pl.when((source >= first) & (source < first + size))
            def _(ref=ref, first=first):
                for copy in packed_copies(ref, lambda e: e - first, plan.block, rope_rows, plan.latent)(source, j, *bufs):
                    what(copy)

    if len(sizes) == 1:
        return every(packed_copies(chunks[0], lambda e: e, plan.block, rope_rows, plan.latent))
    return each


def migrated_kernel(plan, slot, sizes, length, q_lat, q_rope, fresh, *refs):
    chunks, out, scr = refs[: len(sizes)], refs[len(sizes) + 1], refs[len(sizes) + 2 :]
    used = length[0]
    attention(
        plan, scr, own_queries(q_lat.at[slot], q_rope.at[slot], fresh.at[slot]), chunked(plan, sizes, chunks),
        ceil_div(used, plan.block), used, False,
        lambda t, src, sem: pltpu.make_async_copy(src, out.at[slot, t], sem),
    )


def visited_kernel(plan, sizes, length, payload, *refs):
    chunks, out, scr = refs[: len(sizes)], refs[len(sizes)], refs[len(sizes) + 1 :]
    used = length[0]
    attention(
        plan, scr, visiting_queries(payload), chunked(plan, sizes, chunks),
        ceil_div(used, plan.block), used, False,
        lambda t, src, sem: pltpu.make_async_copy(src, out.at[t], sem),
    )


def place_kernel(slot, back, base, out, buf, sem):
    del base
    steps = back.shape[0]
    pulls = [pltpu.make_async_copy(back.at[t], buf.at[t], sem.at[0, t]) for t in range(steps)]
    puts = [pltpu.make_async_copy(buf.at[t], out.at[slot, t], sem.at[1, t]) for t in range(steps)]
    for pull in pulls:
        pull.start()
    for pull, put in zip(pulls, puts, strict=True):
        pull.wait()
        put.start()
    for put in puts:
        put.wait()


def arriving_kernel(plan, slot, index, arrived, q_lat, q_rope, fresh, got, ready, out, rbuf, rsem, *scr):
    fetch = pltpu.make_async_copy(ready, rbuf, rsem.at[0])
    fetch.start()
    used = arrived[0]
    fetch.wait()
    put = pltpu.make_async_copy(rbuf, out.at[slot - 1], rsem.at[1])
    put.start()
    attention(
        plan, scr, own_queries(q_lat.at[slot], q_rope.at[slot], fresh.at[slot]),
        every(packed_copies(got, lambda j: index[j], plan.block, plan.rope * plan.block // plan.latent, plan.latent)),
        used, used * plan.block, True,
        lambda t, src, sem: pltpu.make_async_copy(src, out.at[slot, t], sem),
    )
    put.wait()


def pack_kernel(table, fill, lat, rope, out, lbuf, rbuf, pbuf, lsem, rsem, osem):
    blocks, block, latent = lat.shape
    rows = pbuf.shape[1]
    small = pltpu.make_async_copy(rope, rbuf, rsem)
    pulls = [pltpu.make_async_copy(lat.at[b], lbuf.at[b], lsem.at[b]) for b in range(blocks)]
    small.start()
    for pull in pulls:
        pull.start()
    def each(o, what, src, span, i):
        b = table[o]

        @pl.when(b >= 0)
        def _():
            what(pltpu.make_async_copy(src.at[b], out.at[o, span], osem.at[b, i]))

    top, tail = (lbuf, pl.ds(0, block), 0), (pbuf, pl.ds(block, rows), 1)

    def launch(part):
        def body(o, carry):
            each(o, lambda copy: copy.start(), *part)
            return carry

        lax.fori_loop(0, out.shape[0], body, 0)

    for pull in pulls:
        pull.wait()
    launch(top)
    small.wait()
    first = lax.broadcasted_iota(jnp.int32, rope.shape[1:], 0) == 0
    token = lax.broadcasted_iota(jnp.int32, rope.shape[1:], 1)
    for b in range(blocks):
        marked = jnp.where(first & (token >= fill[b]), MARK, rbuf[b].astype(jnp.float32)).astype(jnp.bfloat16)
        for g in range(latent // block):
            pbuf[b, :, g * block : (g + 1) * block] = marked[g * rows : (g + 1) * rows]
    launch(tail)

    def settle(o, carry):
        each(o, lambda copy: copy.wait(), *top)
        each(o, lambda copy: copy.wait(), *tail)
        return carry

    lax.fori_loop(0, out.shape[0], settle, 0)


def chunk_kernel(spans, slot, lat, rope, q_lat, q_rope, fresh, *refs):
    outs, payload = refs[: len(spans)], refs[len(spans)]
    lbuf, rbuf, pbuf, qbuf, qrbuf, fbuf, mbuf, sem, osem, qsem = refs[len(spans) + 1 :]
    blocks, block, latent = lat.shape
    steps, heads = qbuf.shape[0] // block, block
    rows = pbuf.shape[1]
    wide = steps * heads
    pulls = [
        pltpu.make_async_copy(rope, rbuf, sem.at[0]),
        pltpu.make_async_copy(q_rope.at[slot], qrbuf, sem.at[1]),
        pltpu.make_async_copy(fresh.at[slot], fbuf, sem.at[2]),
        pltpu.make_async_copy(lat, lbuf, sem.at[3]),
    ]
    pulls += [
        pltpu.make_async_copy(q_lat.at[slot, t], qbuf.at[pl.ds(t * heads, heads)], sem.at[4 + t])
        for t in range(steps)
    ]
    for pull in pulls:
        pull.start()
    for pull in pulls:
        pull.wait()
    for b in range(blocks):
        for g in range(latent // block):
            pbuf[b, :, g * block : (g + 1) * block] = rbuf[b, g * rows : (g + 1) * rows]
    puts = []
    for i, ((first, size), out) in enumerate(zip(spans, outs, strict=True)):
        span = pl.ds(first, size)
        puts.append(pltpu.make_async_copy(lbuf.at[span], out.at[:, pl.ds(0, block)], osem.at[i, 0]))
        puts.append(pltpu.make_async_copy(pbuf.at[span], out.at[:, pl.ds(block, rows)], osem.at[i, 1]))
    mbuf[...] = jnp.zeros_like(mbuf)
    new = fbuf[...].astype(jnp.float32)
    mbuf[0:steps, :] = new[:, :latent]
    mbuf[8 : 8 + steps, : new.shape[1] - latent] = new[:, latent:]
    tail = qrbuf.shape[1]
    qbuf[wide + tail : wide + tail + 16, :] = mbuf[...].astype(jnp.bfloat16)
    for t in range(steps):
        qbuf[wide : wide + tail, t * heads : (t + 1) * heads] = qrbuf[t]
    puts.append(pltpu.make_async_copy(qbuf, payload, qsem))
    for put in puts:
        put.start()
    for put in puts:
        put.wait()


def shards(
    res_lat, res_rope, res_table, res_len, out_lat, out_rope, out_fill, send_table, arr_index,
    arr_count, mig_lat, mig_rope, mig_len, mig_bit, q_lat, q_rope, new_kv,
):
    count = lax.axis_size("dp")
    bits = count.bit_length() - 1
    slots, steps, heads, latent = q_lat.shape
    rope = q_rope.shape[2]
    block = res_lat.shape[1]
    requests = res_len.shape[0]
    assert requests == 1 and send_table.shape[0] == count
    make = functools.partial(Plan, steps=steps, heads=heads, latent=latent, rope=rope, block=block)
    rows = rope * block // latent
    blocks = out_lat.shape[0]

    def pack(table, fill, lat, rot):
        return pl.pallas_call(
            pack_kernel,
            out_shape=jax.ShapeDtypeStruct((count, block + rows, latent), jnp.bfloat16),
            in_specs=[SMEM, SMEM, ANY, ANY],
            out_specs=ANY,
            scratch_shapes=[
                pltpu.VMEM((blocks, block, latent), jnp.bfloat16),
                pltpu.VMEM((blocks, rope, block), jnp.bfloat16),
                pltpu.VMEM((blocks, rows, latent), jnp.bfloat16),
                DMA((blocks,)), DMA, DMA((blocks, 2)),
            ],
            cost_estimate=pl.CostEstimate(flops=0, bytes_accessed=8 << 20, transcendentals=0),
            name="pack",
        )(table, fill, lat, rot)

    def swapper(bit):
        route = [(i, i ^ 1 << bit) for i in range(count)]
        return lambda x: lax.ppermute(x, "dp", route)

    def opening(bit):
        return lambda length, *blocks: (swapper(bit)(length), pack(*blocks))

    far = bits - 1
    early, packed = lax.switch(
        mig_bit[0] + 1,
        [lambda length, *blocks: (length, pack(*blocks))] + [opening(bit) for bit in range(bits)],
        mig_len, send_table, out_fill, out_lat, out_rope,
    )
    got = lax.all_to_all(packed, "dp", split_axis=0, concat_axis=0, tiled=True)

    plan = make(res_table.shape[1])
    res_table, packed = lax.optimization_barrier((res_table, packed))
    ready = pl.pallas_call(
        functools.partial(resident_kernel, plan, 0),
        out_shape=jax.ShapeDtypeStruct((steps, heads, latent), jnp.bfloat16),
        in_specs=[SMEM, SMEM, ANY, ANY, ANY, ANY, ANY],
        out_specs=ANY,
        scratch_shapes=plan.scratch(),
        cost_estimate=cost(plan),
        name="resident",
    )(res_table, res_len, q_lat, q_rope, new_kv, res_lat, res_rope)

    held = mig_lat.shape[0]
    sizes = chunk_spans(held)
    levels = [n for n in (2, 4, 6, 8) if n < held]
    mig_lat, mig_rope, packed = lax.optimization_barrier((mig_lat, mig_rope, packed))
    spans = [(sum(sizes[:i]), n) for i, n in enumerate(sizes)] + [(0, n) for n in levels]
    mail = steps * heads + rope + 16
    *pieces, payload = pl.pallas_call(
        functools.partial(chunk_kernel, spans, requests + 1),
        out_shape=[jax.ShapeDtypeStruct((n, block + rows, latent), jnp.bfloat16) for _, n in spans]
        + [jax.ShapeDtypeStruct((mail, latent), jnp.bfloat16)],
        in_specs=[ANY] * 5,
        out_specs=[ANY] * (len(spans) + 1),
        scratch_shapes=[
            pltpu.VMEM((held, block, latent), jnp.bfloat16),
            pltpu.VMEM((held, rope, block), jnp.bfloat16),
            pltpu.VMEM((held, rows, latent), jnp.bfloat16),
            pltpu.VMEM((mail, latent), jnp.bfloat16),
            pltpu.VMEM((steps, rope, heads), jnp.bfloat16),
            pltpu.VMEM(new_kv.shape[1:], jnp.bfloat16),
            pltpu.VMEM((16, latent), jnp.float32),
            DMA((4 + steps,)), DMA((len(spans), 2)), DMA,
        ],
        name="chunk",
    )(mig_lat, mig_rope, q_lat, q_rope, new_kv)
    chunks, prefixes = pieces[: len(sizes)], pieces[len(sizes) :]
    ready, chunks = lax.optimization_barrier((ready, chunks))

    ends = [sum(sizes[: i + 1]) * block for i in range(len(sizes))]
    limit = levels[-1] * block

    def level_of(one, other):
        longest = jnp.maximum(one, other)[0]
        return sum((longest > end).astype(jnp.int32) for end in ends[:-1])

    def near(bit):
        swap = swapper(bit)

        def branch(length, early, chunks, payload):
            other = early

            def sending(k):
                return lambda chunks: [swap(x) if i <= k else x for i, x in enumerate(chunks)]

            if bit < far - 2:
                chunks = lax.switch(level_of(length, other), [sending(k) for k in range(len(sizes))], chunks)
                return other, chunks, payload
            longest = jnp.maximum(length, other)[0]
            most = 1 + sum(end < limit for end in ends)

            def call(k):
                return lambda chunks, payload: (sending(k)(chunks), payload)

            chunks, payload = lax.switch(
                jnp.where(longest > limit, most, level_of(length, other)),
                [call(k) for k in range(most)] + [lambda chunks, payload: (chunks, swap(payload))],
                chunks, payload,
            )
            return other, chunks, payload

        return branch


    def distant(length, early, chunks, payload):
        longest = jnp.maximum(length, early)[0]
        payload = lax.cond(longest > limit, swapper(far), lambda x: x, payload)
        return early, chunks, payload

    length, chunks, payload = lax.switch(
        mig_bit[0] + 1,
        [lambda length, early, chunks, payload: (length, chunks, payload)]
        + [near(bit) for bit in range(far)]
        + [distant],
        mig_len, early, chunks, payload,
    )

    whole = jax.ShapeDtypeStruct((slots, steps, heads, latent), jnp.bfloat16)

    def arrive(index, arrived, got, ready, q_lat, q_rope, new_kv):
        plan = make(index.shape[0])
        return pl.pallas_call(
            functools.partial(arriving_kernel, plan, requests),
            out_shape=whole,
            in_specs=[SMEM, SMEM, ANY, ANY, ANY, ANY, ANY],
            out_specs=ANY,
            scratch_shapes=[pltpu.VMEM((steps, heads, latent), jnp.bfloat16), DMA((2,))] + plan.scratch(),
            cost_estimate=cost(plan),
            name="arriving",
        )(index, arrived, q_lat, q_rope, new_kv, got, ready)

    def migrate(length, q_lat, q_rope, new_kv, sizes, chunks, base):
        plan = make(sum(sizes))
        return pl.pallas_call(
            functools.partial(migrated_kernel, plan, requests + 1, sizes),
            out_shape=whole,
            in_specs=[SMEM] + [ANY] * (4 + len(sizes)),
            out_specs=ANY,
            scratch_shapes=plan.scratch(),
            input_output_aliases={4 + len(sizes): 0},
            cost_estimate=cost(plan),
            name="migrated",
        )(length, q_lat, q_rope, new_kv, *chunks, base)

    swap = swapper(far)

    def local(arrival, queries, own, length, chunks, prefixes, payload):
        base = arrive(*arrival, *queries)
        return migrate(length, *queries, sizes, chunks, base)

    def shipped(k):
        def branch(arrival, queries, own, length, chunks, prefixes, payload):
            cache = swap(prefixes[k])
            base = arrive(*arrival, *queries)
            return migrate(length, *queries, [levels[k]], [cache], base)

        return branch

    def visited(swap, arrival, queries, own, length, chunks, prefixes, payload):
        plan = make(held, visitor=True)
        result = pl.pallas_call(
            functools.partial(visited_kernel, plan, sizes),
            out_shape=jax.ShapeDtypeStruct((steps, heads, latent), jnp.bfloat16),
            in_specs=[SMEM] + [ANY] * (1 + len(sizes)),
            out_specs=ANY,
            scratch_shapes=plan.scratch(),
            cost_estimate=cost(plan),
            name="visited",
        )(own, payload, *chunks)
        back = swap(result)
        base = arrive(*arrival, *queries)
        return pl.pallas_call(
            functools.partial(place_kernel, requests + 1),
            out_shape=whole,
            in_specs=[ANY, ANY],
            out_specs=ANY,
            scratch_shapes=[pltpu.VMEM((steps, heads, latent), jnp.bfloat16), DMA((2, steps))],
            input_output_aliases={1: 0},
            name="place",
        )(back, base)

    longest = jnp.maximum(mig_len, length)[0]
    step = 1 + sum((longest > n * block).astype(jnp.int32) for n in levels)
    bit = mig_bit[0]
    heavy = [b for b in (far, far - 1, far - 2) if b >= 0]
    lower = (bit >= heavy[-1]) & (bit < far) & (longest > limit)
    step = jnp.where(bit == far, step, jnp.where(lower, 1 + len(levels) + far - bit, 0))
    return lax.switch(
        step,
        [local]
        + [shipped(k) for k in range(len(levels))]
        + [functools.partial(visited, swapper(b)) for b in heavy],
        (arr_index, arr_count, got, ready), (q_lat, q_rope, new_kv), mig_len, length, chunks, prefixes, payload,
    )


def solution(mesh):
    whole = P(("groups", "dp"))
    return jax.shard_map(shards, mesh=mesh, in_specs=(whole,) * 17, out_specs=whole, check_vma=False)
```
